256 devices in a mesh: gx: 64 (over x, z_hi, y, core), gy: 4 (over z_lo).
Axes of the slice: x: 4, y: 4, z: 8 (z_hi: 2, z_lo: 4; z = z_hi * 4 + z_lo), core: 2. Of those that a mesh axis runs over, the one named last changes fastest.
Arguments:
- velocity: float32 [3, 512, 64, 512], P(None, 'gx', None, 'gy'), may hold values from -6 to 6
- cotangent: float32 [3, 512, 64, 512], P(None, 'gx', None, 'gy'), may hold values from -6 to 6
- coefficient: float32 [512, 64, 512], P('gx', None, 'gy'), may hold values from 0.5 to 1.5
- level_profile: float32 [64], replicated, may hold values from 0.1 to 1
- vert_deriv: float32 [64, 64], replicated, may hold values from -0.75 to 0.75
- eigen_vectors: float32 [64, 64], replicated, may hold values from -0.75 to 0.75
- eigen_inverse: float32 [64, 64], replicated, may hold values from -0.75 to 0.75
- eigen_rates: float32 [64], replicated, may hold values from 0.25 to 4
Outputs:
- new_velocity: float32 [3, 512, 64, 512], P(None, 'gx', None, 'gy')
- adjoint_velocity: float32 [3, 512, 64, 512], P(None, 'gx', None, 'gy')
- viscosity_gradient: float32 [512, 64, 512], P('gx', None, 'gy')
The draws below stay inside these ranges and needn't reach their ends.
All inputs are finite; a program needn't handle non-finite values.
Results may differ from the reference program's by a relative error of at most 0.00005.
Values sent between devices are 32-bit elements; how exact they have to be, the bound alone decides.
A program may use at most 128 MiB of HBM per device.

```python
import math
import jax
import jax.numpy as jnp
from jax import lax

NX = 512
NY = 512
NZ = 64


def level_of(stream_key, dims, pieces, smallest, largest):
    def one(position, blocks):
        heights = jax.random.uniform(jax.random.fold_in(jax.random.fold_in(stream_key, 6), position), (blocks,), jnp.float32, smallest / len(pieces), largest / len(pieces))
        return jnp.repeat(jnp.exp(heights), dims[position] // blocks).reshape((-1,) + (1,) * (len(dims) - position - 1))

    loudness = one(*pieces[0])
    for cut in pieces[1:]:
        loudness = loudness * one(*cut)
    return loudness


def gaussian(rng, dims, deviation, limit, split=(), kind=jnp.bfloat16):
    array = deviation * jax.random.normal(rng, dims, jnp.float32)
    if split:
        array = array * level_of(rng, dims, split, -0.22, 0.18)
    return jnp.clip(array, -limit, limit).astype(kind)


def setup_inputs(seed: int = 0) -> dict:
    arg_keys = jax.random.split(jax.random.key(seed), 9)
    velocity = gaussian(arg_keys[0], (3, NX, NZ, NY), 1.0, 6.0, ((1, 64), (3, 4)), jnp.float32)
    cotangent = gaussian(arg_keys[1], (3, NX, NZ, NY), 1.0, 6.0, ((1, 64), (3, 4)), jnp.float32)
    coefficient = jnp.clip(0.5 + 1.0 * jax.random.uniform(arg_keys[2], (NX, NZ, NY), jnp.float32) ** level_of(arg_keys[2], (NX, NZ, NY), ((0, 64), (2, 4)), -0.2, 0.2), 0.5, 1.5)
    level_profile = jnp.clip(jnp.exp(jax.random.uniform(arg_keys[3], (NZ,), jnp.float32, math.log(0.1), math.log(1.0))), 0.1, 1.0)
    vert_deriv = gaussian(arg_keys[4], (NZ, NZ), NZ ** -0.5, 0.75, (), jnp.float32)
    eigen_vectors = gaussian(arg_keys[5], (NZ, NZ), NZ ** -0.5, 0.75, (), jnp.float32)
    eigen_inverse = gaussian(arg_keys[6], (NZ, NZ), NZ ** -0.5, 0.75, (), jnp.float32)
    eigen_rates = jnp.clip(jnp.exp(jax.random.uniform(arg_keys[7], (NZ,), jnp.float32, math.log(0.25), math.log(4.0))), 0.25, 4.0)
    return dict(velocity=velocity, cotangent=cotangent, coefficient=coefficient, level_profile=level_profile, vert_deriv=vert_deriv, eigen_vectors=eigen_vectors, eigen_inverse=eigen_inverse, eigen_rates=eigen_rates)


step_weight = 0.3 * 8.0 / 15.0
precise = lax.Precision.HIGHEST


def levels(matrix, field):
    return jnp.einsum('mz,xzy->xmy', matrix, field, precision=precise)


def wavenumbers(count):
    modes = jnp.arange(count, dtype=jnp.int32)
    signed = jnp.where(modes < count // 2, modes, modes - count)
    signed = jnp.where(modes == count // 2, jnp.zeros_like(signed), signed)
    return signed.astype(jnp.float32) * (2.0 * math.pi / count)


def spectral(fields, eigen_rates):
    spectra = jnp.fft.fft2(fields, axes=(1, 3))
    wave_x = wavenumbers(NX)[:, None, None]
    wave_y = wavenumbers(NY)[None, None, :]
    diverg = 1j * wave_x * spectra[0] + 1j * wave_y * spectra[1] + spectra[2]
    factor = -1.0 / (eigen_rates[None, :, None] + wave_x * wave_x + wave_y * wave_y)
    solved = factor * diverg
    terms = jnp.stack([1j * wave_x * solved, 1j * wave_y * solved, solved])
    inverse = jnp.fft.ifft2(terms, axes=(1, 3))
    return jnp.real(inverse).astype(fields.dtype)


def reference(velocity, cotangent, coefficient, level_profile, vert_deriv, eigen_vectors, eigen_inverse, eigen_rates):
    east = jnp.roll(velocity, -1, axis=1)
    west = jnp.roll(velocity, 1, axis=1)
    north = jnp.roll(velocity, -1, axis=3)
    south = jnp.roll(velocity, 1, axis=3)
    slope_x = 0.5 * (east - west)
    slope_y = 0.5 * (north - south)
    laplace = east + west + north + south - 4.0 * velocity
    slope_z = jnp.einsum('mz,cxzy->cxmy', vert_deriv, velocity, precision=precise)
    advect = -(velocity[0] * slope_x + velocity[1] * slope_y + velocity[2] * slope_z)
    viscosity = coefficient * level_profile[None, :, None]
    section = velocity + step_weight * (advect + viscosity * laplace)
    forward_in = jnp.stack([levels(eigen_inverse, section[0]), levels(eigen_inverse, section[1]),
                            levels(eigen_inverse, levels(vert_deriv, section[2]))])
    forward_out = spectral(forward_in, eigen_rates)
    pressure = jnp.stack([levels(eigen_vectors, forward_out[0]), levels(eigen_vectors, forward_out[1]),
                          levels(vert_deriv, levels(eigen_vectors, forward_out[2]))])
    new_velocity = section - pressure
    vectors_t = eigen_vectors.T
    inverse_t = eigen_inverse.T
    deriv_t = vert_deriv.T
    adjoint_in = jnp.stack([-levels(vectors_t, cotangent[0]), -levels(vectors_t, cotangent[1]),
                            levels(vectors_t, levels(deriv_t, cotangent[2]))])
    adjoint_out = spectral(adjoint_in, eigen_rates)
    adjoint_velocity = cotangent + jnp.stack([levels(inverse_t, adjoint_out[0]), levels(inverse_t, adjoint_out[1]),
                                              -levels(deriv_t, levels(inverse_t, adjoint_out[2]))])
    gradient = step_weight * level_profile[None, :, None] * jnp.sum(adjoint_velocity * laplace, axis=0)
    return new_velocity, adjoint_velocity, gradient
```

```python
import functools
import math

import jax
import jax.numpy as jnp
import ml_dtypes
import numpy as np
from jax import lax
from jax.experimental import pallas as pl
from jax.experimental.pallas import tpu as pltpu
from jax.sharding import PartitionSpec as P

MESH = pl.DeviceIdType.MESH
step_weight = 0.3 * 8.0 / 15.0
N = 512
HALF = N // 2
UNIT = 2.0 * math.pi / N
f32 = jnp.float32
bf16 = jnp.bfloat16


def basis():
    k = np.arange(HALF)[:, None]
    x = np.arange(N)[None, :]
    angle = (k * x % N) * (2.0 * np.pi / N)
    cos, sin = np.cos(angle), np.sin(angle)
    sin[0] = np.cos(np.pi * x[0])
    scale = np.full((HALF, 1), math.sqrt(2.0 / N))
    scale[0] = math.sqrt(1.0 / N)
    table = np.concatenate([scale * cos, scale * sin], axis=0)
    out = []
    for t in (table, table.T):
        high = t.astype(ml_dtypes.bfloat16)
        low = (t - high.astype(np.float64)).astype(ml_dtypes.bfloat16)
        out += [np.ascontiguousarray(high), np.ascontiguousarray(low)]
    return out


def split(v):
    high = v.astype(bf16)
    return high, (v - high.astype(f32)).astype(bf16)


def dot(a, b):
    return jnp.dot(a, b, preferred_element_type=f32)


def dot3(a_high, a_low, b_high, b_low):
    return dot(a_high, b_high) + (dot(a_high, b_low) + dot(a_low, b_high))


def lanes(shape):
    return lax.broadcasted_iota(jnp.int32, shape, len(shape) - 1)


def quad(m):
    high, low = split(m)
    odd = (lanes(m.shape) // 64) % 2 == 1
    return jnp.where(odd, low.astype(f32), high.astype(f32)).astype(bf16)


def apply(m4, f):
    high, low = split(f)
    return dot(m4, jnp.concatenate([high, high, low, low], axis=0))


def body_kernel(
    vel, cot, coef, prof, mats, rates, t_high, t_low, tt_high, tt_low,
    o_new, o_adj, o_grad,
    velp, cotv, coefv, lap, sec, grad, ycol, yhalo,
    send_z, recv_x, back_x, back_z, grp, grp_in, bck, bck_in,
    tab, ttab, m4,
    load_sem, out_sem, hx_send, hx_recv, hy_send, hy_recv,
    big_send, big_recv, grp_send, grp_recv, bck_send, bck_recv, ret_send, ret_recv,
):
    gx = lax.axis_index("gx")
    q = lax.axis_index("gy")
    core = gx % 2
    cy = (gx // 2) % 4
    cx = gx // 16
    cz = ((gx // 8) % 2) * 4 + q
    part = (cy % 2) * 2 + core
    level = (cx * 2 + cy // 2) * 8 + cz

    def gx_of(x, z, y, c):
        return ((x * 2 + z // 4) * 4 + y) * 2 + c

    def member(j):
        return (gx_of(cx, cz, (cy // 2) * 2 + j // 2, j % 2), q)

    east, west = ((gx + 1) % 64, q), ((gx + 63) % 64, q)
    north, south = (gx, (q + 1) % 4), (gx, (q + 3) % 4)

    barrier = pltpu.get_barrier_semaphore()

    def tell(dev):
        pl.semaphore_signal(barrier, inc=1, device_id=dev, device_id_type=MESH)

    def tell_source(t, carry):
        i = (gx + t) % 64

        @pl.when(jnp.logical_or(i != gx, q != part))
        def _():
            tell((i, part))

        return carry

    lax.fori_loop(0, 64, tell_source, 0)
    for d in range(1, 4):
        tell(member((part + d) % 4))
    for dev in (east, west, north, south):
        tell(dev)

    loads = [
        pltpu.make_async_copy(cot, cotv, load_sem.at[0]),
        pltpu.make_async_copy(vel, velp.at[:, pl.ds(1, 8)], load_sem.at[1]),
        pltpu.make_async_copy(coef, coefv, load_sem.at[2]),
        pltpu.make_async_copy(t_high, tab.at[0], load_sem.at[3]),
        pltpu.make_async_copy(t_low, tab.at[1], load_sem.at[4]),
        pltpu.make_async_copy(tt_high, ttab.at[0], load_sem.at[5]),
        pltpu.make_async_copy(tt_low, ttab.at[1], load_sem.at[6]),
    ]
    for copy in loads:
        copy.start()

    D, V, E, Dt, Vt, Et = (mats[i] for i in range(6))
    qD, qV, qE, qDt, qVt, qEt = (quad(m) for m in (D, V, E, Dt, Vt, Et))
    m4[0] = quad(-Vt)
    m4[1] = quad(apply(qVt, Dt))
    m4[2] = qD
    m4[3] = qE
    m4[4] = quad(apply(qE, D))
    m4[5] = qEt
    m4[6] = quad(-apply(qDt, Et))
    m4[7] = qV
    m4[8] = quad(apply(qD, V))

    loads[0].wait()

    def adjoint_in(xp, carry):
        x = xp * 2
        for c in range(3):
            f = jnp.concatenate([cotv[c, x], cotv[c, x + 1]], axis=1)
            g = apply(m4[1 if c == 2 else 0], f)
            send_z[0, pl.ds(c * 8 + x, 64, stride=24), :] = g[:, :128]
            send_z[0, pl.ds(c * 8 + x + 1, 64, stride=24), :] = g[:, 128:]
        return carry

    lax.fori_loop(0, 4, adjoint_in, 0)

    loads[1].wait()
    lane = lanes((64, 128))

    def pack(x, carry):
        first, last = carry
        for c in range(3):
            f = velp[c, x + 1]
            j = c * 8 + x
            first = jnp.where(lane == j, pltpu.roll(f, j, 1), first)
            last = jnp.where(lane == j, pltpu.roll(f, j + 1, 1), last)
        return first, last

    zero = jnp.zeros((64, 128), f32)
    first, last = lax.fori_loop(0, 8, pack, (zero, zero))
    ycol[0] = first
    ycol[1] = last

    @pl.when(q == part)
    def _():
        pl.semaphore_wait(barrier, 70)

    @pl.when(q != part)
    def _():
        pl.semaphore_wait(barrier, 71)

    def remote(src, dst, ssem, rsem, dev):
        return pltpu.make_async_remote_copy(
            src_ref=src, dst_ref=dst, send_sem=ssem, recv_sem=rsem,
            device_id=dev, device_id_type=MESH,
        )

    halos = [
        remote(velp.at[:, 8], velp.at[:, 0], hx_send.at[0], hx_recv.at[0], east),
        remote(velp.at[:, 1], velp.at[:, 9], hx_send.at[1], hx_recv.at[1], west),
        remote(ycol.at[1], yhalo.at[0], hy_send.at[0], hy_recv.at[0], north),
        remote(ycol.at[0], yhalo.at[1], hy_send.at[1], hy_recv.at[1], south),
    ]
    for copy in halos:
        copy.start()

    def send_levels(e):
        def go(t, carry):
            dz = t % 8
            dx = (t // 8) % 4
            dy = t // 32
            off = (dz % 2) * (4 - (dz + 1) // 2) + (1 - dz % 2) * (4 + dz // 2)
            z = (cz + off) % 8
            x = (cx + dx) % 4
            h = (cy // 2 + dy) % 2
            target = gx_of(x, z, h * 2 + q // 2, q % 2)
            home = (x * 2 + h) * 8 + z
            src = send_z.at[e, pl.ds(pl.multiple_of(home * 24, 8), 24), :]
            dst = recv_x.at[e, gx]
            mine = jnp.logical_and(home == level, q == part)

            @pl.when(mine)
            def _():
                pltpu.make_async_copy(src, dst, big_recv.at[e]).start()

            @pl.when(jnp.logical_not(mine))
            def _():
                remote(src, dst, big_send.at[e], big_recv.at[e], (target, z % 4)).start()

            return carry

        lax.fori_loop(0, 64, go, 0)

    def send_columns(e):
        def go(t, carry):
            h = t % 2
            c = (core + (t // 2) % 2) % 2
            x = (cx + (t // 4) % 4) % 4
            y = (cy + t // 16) % 4
            i = gx_of(x, h * 4, y, c)
            src = back_x.at[e, i]
            dst = back_z.at[e, pl.ds(pl.multiple_of(level * 24, 8), 24), :]
            mine = jnp.logical_and(i == gx, q == part)

            @pl.when(mine)
            def _():
                pltpu.make_async_copy(src, dst, ret_recv.at[e]).start()

            @pl.when(jnp.logical_not(mine))
            def _():
                remote(src, dst, ret_send.at[e], ret_recv.at[e], (i, part)).start()

            return carry

        lax.fori_loop(0, 64, go, 0)

    def all_of(ref, sem):
        pltpu.make_async_copy(ref, ref, sem).wait()

    def swap(e, out, into, ssem, rsem):
        for d in range(1, 4):
            j = (part + d) % 4
            remote(out.at[e, j], into.at[e, part], ssem.at[e], rsem.at[e], member(j)).start()
        pltpu.make_async_copy(out.at[e, part], into.at[e, part], rsem.at[e]).start()

    send_levels(0)

    halos[0].wait_recv()
    halos[1].wait_recv()
    halos[2].wait_recv()
    halos[3].wait_recv()
    loads[2].wait()
    profile = prof[...]

    def section(xp, carry):
        pair = []
        for x in (xp * 2, xp * 2 + 1):
            here = [velp[c, x + 1] for c in range(3)]
            rows = []
            for c in range(3):
                f = here[c]
                e, w = velp[c, x + 2], velp[c, x]
                j = c * 8 + x
                n = jnp.where(lane == 127, pltpu.roll(yhalo[1], 127 - j, 1), pltpu.roll(f, 127, 1))
                s = jnp.where(lane == 0, pltpu.roll(yhalo[0], (128 - j) % 128, 1), pltpu.roll(f, 1, 1))
                laplace = e + w + n + s - 4.0 * f
                lap[c, x] = laplace
                move = here[0] * (0.5 * (e - w)) + here[1] * (0.5 * (n - s))
                rows.append(f + step_weight * (coefv[x] * profile * laplace - move))
            pair.append((here, rows))
        for c in range(3):
            f = jnp.concatenate([pair[0][0][c], pair[1][0][c]], axis=1)
            slope = apply(m4[2], f)
            s = []
            for k in range(2):
                here, rows = pair[k]
                v = rows[c] - step_weight * (here[2] * slope[:, k * 128 : (k + 1) * 128])
                sec[c, xp * 2 + k] = v
                s.append(v)
            g = apply(m4[4 if c == 2 else 3], jnp.concatenate(s, axis=1))
            send_z[1, pl.ds(c * 8 + xp * 2, 64, stride=24), :] = g[:, :128]
            send_z[1, pl.ds(c * 8 + xp * 2 + 1, 64, stride=24), :] = g[:, 128:]
        return carry

    lax.fori_loop(0, 4, section, 0)
    send_levels(1)

    for copy in loads[3:]:
        copy.wait()

    kx_all = lax.broadcasted_iota(jnp.int32, (HALF, 128), 0).astype(f32) * UNIT

    def into_modes(e):
        all_of(recv_x.at[e], big_recv.at[e])
        g = [recv_x[e, :, c * 8 : (c + 1) * 8, :].reshape(N, 128) for c in range(3)]
        high, low = split(jnp.concatenate(g, axis=1))
        modes = dot3(tab[0], tab[1], high, low)
        c0, s0 = modes[:HALF, :128], modes[HALF:, :128]
        uc = modes[:HALF, 256:] + kx_all * s0
        us = modes[HALF:, 256:] - kx_all * c0
        vc, vs = modes[:HALF, 128:256], modes[HALF:, 128:256]
        for j in range(4):
            for r, block in enumerate((uc, us, vc, vs)):
                grp[e, j, r * 64 : (r + 1) * 64, :] = block[j * 64 : (j + 1) * 64]
        swap(e, grp, grp_in, grp_send, grp_recv)

    rate = rates[level]

    def solve(e):
        all_of(grp_in.at[e], grp_recv.at[e])
        high, low = split(jnp.concatenate([grp_in[e, j] for j in range(4)], axis=1))
        spec = dot3(high, low, ttab[0], ttab[1])
        row = lax.broadcasted_iota(jnp.int32, (128, HALF), 0) % 64 + part * 64
        kx = row.astype(f32) * UNIT
        ky = lanes((128, HALF)).astype(f32) * UNIT
        factor = -1.0 / (rate + kx * kx + ky * ky)
        pc = factor * (spec[:128, :HALF] + ky * spec[128:, HALF:])
        ps = factor * (spec[:128, HALF:] - ky * spec[128:, :HALF])
        both = jnp.concatenate(
            [
                jnp.concatenate([pc, ps], axis=1),
                jnp.concatenate([ky * ps, -(ky * pc)], axis=1),
            ],
            axis=0,
        )
        high, low = split(both)
        out = dot3(high, low, tab[0], tab[1])
        for j in range(4):
            bck[e, j] = out[:, j * 128 : (j + 1) * 128]
        swap(e, bck, bck_in, bck_send, bck_recv)

    def from_modes(e):
        all_of(bck_in.at[e], bck_recv.at[e])
        r = [
            jnp.concatenate([bck_in[e, j, k * 64 : (k + 1) * 64, :] for j in range(4)], axis=0)
            for k in range(4)
        ]
        pc, ps, yc, ys = r
        rhs = jnp.concatenate(
            [
                jnp.concatenate([kx_all * ps, yc, pc], axis=1),
                jnp.concatenate([-(kx_all * pc), ys, ps], axis=1),
            ],
            axis=0,
        )
        high, low = split(rhs)
        out = dot3(ttab[0], ttab[1], high, low)
        for c in range(3):
            back_x[e, :, c * 8 : (c + 1) * 8, :] = out[:, c * 128 : (c + 1) * 128].reshape(64, 8, 128)
        send_columns(e)

    into_modes(0)
    into_modes(1)
    solve(0)
    solve(1)
    from_modes(0)
    from_modes(1)

    all_of(back_z.at[0], ret_recv.at[0])

    def levels_of(e, c, x):
        return jnp.concatenate(
            [
                back_z[e, pl.ds(c * 8 + x, 64, stride=24), :],
                back_z[e, pl.ds(c * 8 + x + 1, 64, stride=24), :],
            ],
            axis=1,
        )

    def adjoint_out(xp, carry):
        x = xp * 2
        total = [zero, zero]
        for c in range(3):
            g = apply(m4[6 if c == 2 else 5], levels_of(0, c, x))
            for k in range(2):
                v = cotv[c, x + k] + g[:, k * 128 : (k + 1) * 128]
                cotv[c, x + k] = v
                total[k] = total[k] + v * lap[c, x + k]
        for k in range(2):
            grad[x + k] = step_weight * profile * total[k]
        return carry

    lax.fori_loop(0, 4, adjoint_out, 0)
    outs = [
        pltpu.make_async_copy(cotv, o_adj, out_sem.at[0]),
        pltpu.make_async_copy(grad, o_grad, out_sem.at[1]),
        pltpu.make_async_copy(sec, o_new, out_sem.at[2]),
    ]
    outs[0].start()
    outs[1].start()

    all_of(back_z.at[1], ret_recv.at[1])

    def forward_out(xp, carry):
        x = xp * 2
        for c in range(3):
            g = apply(m4[8 if c == 2 else 7], levels_of(1, c, x))
            for k in range(2):
                sec[c, x + k] = sec[c, x + k] - g[:, k * 128 : (k + 1) * 128]
        return carry

    lax.fori_loop(0, 4, forward_out, 0)
    outs[2].start()

    for copy in halos:
        copy.wait_send()
    for e in range(2):

        @pl.when(q == part)
        def _():
            all_of(recv_x.at[e, pl.ds(0, 63)], big_send.at[e])
            all_of(recv_x.at[e, pl.ds(0, 63)], ret_send.at[e])

        @pl.when(q != part)
        def _():
            all_of(recv_x.at[e], big_send.at[e])
            all_of(recv_x.at[e], ret_send.at[e])

        all_of(grp.at[e, pl.ds(0, 3)], grp_send.at[e])
        all_of(bck.at[e, pl.ds(0, 3)], bck_send.at[e])
    for copy in outs:
        copy.wait()


def body(velocity, cotangent, coefficient, level_profile, vert_deriv, eigen_vectors, eigen_inverse, eigen_rates):
    squares = jnp.stack([vert_deriv, eigen_vectors, eigen_inverse])
    mats = jnp.tile(jnp.concatenate([squares, jnp.swapaxes(squares, 1, 2)], axis=0), (1, 1, 4))
    profile = jnp.broadcast_to(level_profile[:, None], (64, 128))
    tables = [jnp.asarray(t) for t in basis()]
    hbm = pl.BlockSpec(memory_space=pl.ANY)
    vmem = pl.BlockSpec(memory_space=pltpu.VMEM)
    smem = pl.BlockSpec(memory_space=pltpu.SMEM)
    field = (3, 8, 64, 128)
    dma = pltpu.SemaphoreType.DMA
    return pl.pallas_call(
        body_kernel,
        out_shape=(
            jax.ShapeDtypeStruct(field, f32),
            jax.ShapeDtypeStruct(field, f32),
            jax.ShapeDtypeStruct(field[1:], f32),
        ),
        in_specs=[hbm, hbm, hbm, vmem, vmem, smem, hbm, hbm, hbm, hbm],
        out_specs=(hbm, hbm, hbm),
        scratch_shapes=[
            pltpu.VMEM((3, 10, 64, 128), f32),
            pltpu.VMEM(field, f32),
            pltpu.VMEM(field[1:], f32),
            pltpu.VMEM(field, f32),
            pltpu.VMEM(field, f32),
            pltpu.VMEM(field[1:], f32),
            pltpu.VMEM((2, 64, 128), f32),
            pltpu.VMEM((2, 64, 128), f32),
            pltpu.VMEM((2, 1536, 128), f32),
            pltpu.VMEM((2, 64, 24, 128), f32),
            pltpu.VMEM((2, 64, 24, 128), f32),
            pltpu.VMEM((2, 1536, 128), f32),
            pltpu.VMEM((2, 4, 256, 128), f32),
            pltpu.VMEM((2, 4, 256, 128), f32),
            pltpu.VMEM((2, 4, 256, 128), f32),
            pltpu.VMEM((2, 4, 256, 128), f32),
            pltpu.VMEM((2, N, N), bf16),
            pltpu.VMEM((2, N, N), bf16),
            pltpu.VMEM((9, 64, 256), bf16),
            dma((7,)),
            dma((3,)),
            dma((2,)), dma((2,)), dma((2,)), dma((2,)),
            dma((2,)), dma((2,)), dma((2,)), dma((2,)),
            dma((2,)), dma((2,)), dma((2,)), dma((2,)),
        ],
        compiler_params=pltpu.CompilerParams(
            collective_id=0, has_side_effects=True, vmem_limit_bytes=56 << 20
        ),
        name="substep",
    )(velocity, cotangent, coefficient, profile, mats, eigen_rates, *tables)


def solution(mesh):
    field = P(None, "gx", None, "gy")
    cell = P("gx", None, "gy")
    in_specs = (field, field, cell, P(), P(), P(), P(), P())
    return jax.shard_map(body, mesh=mesh, in_specs=in_specs, out_specs=(field, field, cell), check_vma=False)
```

```python
import functools
import math

import jax
import jax.numpy as jnp
import ml_dtypes
import numpy as np
from jax import lax
from jax.experimental import pallas as pl
from jax.experimental.pallas import tpu as pltpu
from jax.sharding import PartitionSpec as P

MESH = pl.DeviceIdType.MESH
step_weight = 0.3 * 8.0 / 15.0
N = 512
CUT_F = 32
CUT_R = 32
HALF = N // 2
UNIT = 2.0 * math.pi / N
f32 = jnp.float32
bf16 = jnp.bfloat16


def basis():
    k = np.arange(HALF)[:, None]
    x = np.arange(N)[None, :]
    angle = (k * x % N) * (2.0 * np.pi / N)
    cos, sin = np.cos(angle), np.sin(angle)
    sin[0] = np.cos(np.pi * x[0])
    scale = np.full((HALF, 1), math.sqrt(2.0 / N))
    scale[0] = math.sqrt(1.0 / N)
    table = np.concatenate([scale * cos, scale * sin], axis=0)
    out = []
    for t in (table, table.T):
        high = t.astype(ml_dtypes.bfloat16)
        low = (t - high.astype(np.float64)).astype(ml_dtypes.bfloat16)
        out += [np.ascontiguousarray(high), np.ascontiguousarray(low)]
    return out


def split(v):
    high = v.astype(bf16)
    return high, (v - high.astype(f32)).astype(bf16)


def dot(a, b):
    return jnp.dot(a, b, preferred_element_type=f32)


def dot3(a_high, a_low, b_high, b_low):
    return dot(a_high, b_high) + (dot(a_high, b_low) + dot(a_low, b_high))


def lanes(shape):
    return lax.broadcasted_iota(jnp.int32, shape, len(shape) - 1)


def quad(m):
    high, low = split(m)
    odd = (lanes(m.shape) // 64) % 2 == 1
    return jnp.where(odd, low.astype(f32), high.astype(f32)).astype(bf16)


def apply(m4, f):
    high, low = split(f)
    return dot(m4, jnp.concatenate([high, high, low, low], axis=0))


def body_kernel(
    vel, cot, coef, prof, mats, rates, t_high, t_low, tt_high, tt_low,
    o_new, o_adj, o_grad,
    velp, cotv, coefv, lap, sec, grad, ycol, yhalo,
    send_z, recv_x, back_x, back_z, grp, grp_in, bck, bck_in,
    tab, ttab, m4,
    load_sem, out_sem, hx_send, hx_recv, hy_send, hy_recv,
    big_send, big_recv, grp_send, grp_recv, bck_send, bck_recv, ret_send, ret_recv,
):
    gx = lax.axis_index("gx")
    q = lax.axis_index("gy")
    core = gx % 2
    cy = (gx // 2) % 4
    cx = gx // 16
    cz = ((gx // 8) % 2) * 4 + q
    part = ((cy + cz) % 2) * 2 + core
    level = (cx * 2 + cy // 2) * 8 + cz

    def gx_of(x, z, y, c):
        return ((x * 2 + z // 4) * 4 + y) * 2 + c

    def member(j):
        return (gx_of(cx, cz, (cy // 2) * 2 + (j // 2 + cz) % 2, j % 2), q)

    east, west = ((gx + 1) % 64, q), ((gx + 63) % 64, q)
    north, south = (gx, (q + 1) % 4), (gx, (q + 3) % 4)

    barrier = pltpu.get_barrier_semaphore()

    def tell(dev):
        pl.semaphore_signal(barrier, inc=1, device_id=dev, device_id_type=MESH)

    def tell_source(t, carry):
        i = (gx + t) % 64

        @pl.when(jnp.logical_or(i != gx, q != part))
        def _():
            tell((i, part))

        return carry

    lax.fori_loop(0, 64, tell_source, 0)
    for d in range(1, 4):
        tell(member((part + d) % 4))
    for dev in (east, west, north, south):
        tell(dev)

    loads = [
        pltpu.make_async_copy(cot, cotv, load_sem.at[0]),
        pltpu.make_async_copy(vel, velp.at[:, pl.ds(1, 8)], load_sem.at[1]),
        pltpu.make_async_copy(coef, coefv, load_sem.at[2]),
        pltpu.make_async_copy(t_high, tab.at[0], load_sem.at[3]),
        pltpu.make_async_copy(t_low, tab.at[1], load_sem.at[4]),
        pltpu.make_async_copy(tt_high, ttab.at[0], load_sem.at[5]),
        pltpu.make_async_copy(tt_low, ttab.at[1], load_sem.at[6]),
    ]
    for copy in loads:
        copy.start()

    D, V, E, Dt, Vt, Et = (mats[i] for i in range(6))
    qD, qV, qE, qDt, qVt, qEt = (quad(m) for m in (D, V, E, Dt, Vt, Et))
    m4[0] = quad(-Vt)
    m4[1] = quad(apply(qVt, Dt))
    m4[2] = qD
    m4[3] = qE
    m4[4] = quad(apply(qE, D))
    m4[5] = qEt
    m4[6] = quad(-apply(qDt, Et))
    m4[7] = qV
    m4[8] = quad(apply(qD, V))

    loads[0].wait()

    def adjoint_in(xp, carry):
        x = xp * 2
        for c in range(3):
            f = jnp.concatenate([cotv[c, x], cotv[c, x + 1]], axis=1)
            g = apply(m4[1 if c == 2 else 0], f)
            send_z[0, pl.ds(c * 8 + x, 64, stride=24), :] = g[:, :128]
            send_z[0, pl.ds(c * 8 + x + 1, 64, stride=24), :] = g[:, 128:]
        return carry

    lax.fori_loop(0, 4, adjoint_in, 0)

    loads[1].wait()
    lane = lanes((64, 128))

    def pack(x, carry):
        first, last = carry
        for c in range(3):
            f = velp[c, x + 1]
            j = c * 8 + x
            first = jnp.where(lane == j, pltpu.roll(f, j, 1), first)
            last = jnp.where(lane == j, pltpu.roll(f, j + 1, 1), last)
        return first, last

    zero = jnp.zeros((64, 128), f32)
    first, last = lax.fori_loop(0, 8, pack, (zero, zero))
    ycol[0] = first
    ycol[1] = last

    @pl.when(q == part)
    def _():
        pl.semaphore_wait(barrier, 70)

    @pl.when(q != part)
    def _():
        pl.semaphore_wait(barrier, 71)

    def remote(src, dst, ssem, rsem, dev):
        return pltpu.make_async_remote_copy(
            src_ref=src, dst_ref=dst, send_sem=ssem, recv_sem=rsem,
            device_id=dev, device_id_type=MESH,
        )

    halos = [
        remote(velp.at[:, 8], velp.at[:, 0], hx_send.at[0], hx_recv.at[0], east),
        remote(velp.at[:, 1], velp.at[:, 9], hx_send.at[1], hx_recv.at[1], west),
        remote(ycol.at[1], yhalo.at[0], hy_send.at[0], hy_recv.at[0], north),
        remote(ycol.at[0], yhalo.at[1], hy_send.at[1], hy_recv.at[1], south),
    ]
    for copy in halos:
        copy.start()

    def send_levels(e, start=0, stop=64):
        def go(t, carry):
            dz = t % 8
            u = (t // 8 + 2 * part) % 8
            dx = u % 4
            dy = u // 4
            off = (dz % 2) * (4 - (dz + 1) // 2) + (1 - dz % 2) * (4 + dz // 2)
            z = (cz + off) % 8
            x = (cx + dx) % 4
            h = (cy // 2 + dy) % 2
            target = gx_of(x, z, h * 2 + (q // 2 + z) % 2, q % 2)
            home = (x * 2 + h) * 8 + z
            src = send_z.at[e, pl.ds(pl.multiple_of(home * 24, 8), 24), :]
            dst = recv_x.at[e, gx]
            mine = jnp.logical_and(home == level, q == part)

            @pl.when(mine)
            def _():
                pltpu.make_async_copy(src, dst, big_recv.at[e]).start()

            @pl.when(jnp.logical_not(mine))
            def _():
                remote(src, dst, big_send.at[e], big_recv.at[e], (target, z % 4)).start()

            return carry

        lax.fori_loop(start, stop, go, 0)

    def send_columns(e, start=0, stop=64):
        def go(t, carry):
            u = (t + 8 * cz) % 64
            h = u % 2
            c = (core + (u // 2) % 2) % 2
            x = (cx + (u // 4) % 4) % 4
            y = (cy + u // 16) % 4
            i = gx_of(x, h * 4, y, c)
            src = back_x.at[e, i]
            dst = back_z.at[e, pl.ds(pl.multiple_of(level * 24, 8), 24), :]
            mine = jnp.logical_and(i == gx, q == part)

            @pl.when(mine)
            def _():
                pltpu.make_async_copy(src, dst, ret_recv.at[e]).start()

            @pl.when(jnp.logical_not(mine))
            def _():
                remote(src, dst, ret_send.at[e], ret_recv.at[e], (i, part)).start()

            return carry

        lax.fori_loop(start, stop, go, 0)

    def all_of(ref, sem):
        pltpu.make_async_copy(ref, ref, sem).wait()

    def swap(e, out, into, ssem, rsem):
        for d in range(1, 4):
            j = (part + d) % 4
            remote(out.at[e, j], into.at[e, part], ssem.at[e], rsem.at[e], member(j)).start()
        pltpu.make_async_copy(out.at[e, part], into.at[e, part], rsem.at[e]).start()

    send_levels(0)

    halos[0].wait_recv()
    halos[1].wait_recv()
    halos[2].wait_recv()
    halos[3].wait_recv()
    loads[2].wait()
    profile = prof[...]

    def section(xp, carry):
        pair = []
        for x in (xp * 2, xp * 2 + 1):
            here = [velp[c, x + 1] for c in range(3)]
            rows = []
            for c in range(3):
                f = here[c]
                e, w = velp[c, x + 2], velp[c, x]
                j = c * 8 + x
                n = jnp.where(lane == 127, pltpu.roll(yhalo[1], 127 - j, 1), pltpu.roll(f, 127, 1))
                s = jnp.where(lane == 0, pltpu.roll(yhalo[0], (128 - j) % 128, 1), pltpu.roll(f, 1, 1))
                laplace = e + w + n + s - 4.0 * f
                lap[c, x] = laplace
                move = here[0] * (0.5 * (e - w)) + here[1] * (0.5 * (n - s))
                rows.append(f + step_weight * (coefv[x] * profile * laplace - move))
            pair.append((here, rows))
        for c in range(3):
            f = jnp.concatenate([pair[0][0][c], pair[1][0][c]], axis=1)
            slope = apply(m4[2], f)
            s = []
            for k in range(2):
                here, rows = pair[k]
                v = rows[c] - step_weight * (here[2] * slope[:, k * 128 : (k + 1) * 128])
                sec[c, xp * 2 + k] = v
                s.append(v)
            g = apply(m4[4 if c == 2 else 3], jnp.concatenate(s, axis=1))
            send_z[1, pl.ds(c * 8 + xp * 2, 64, stride=24), :] = g[:, :128]
            send_z[1, pl.ds(c * 8 + xp * 2 + 1, 64, stride=24), :] = g[:, 128:]
        return carry

    lax.fori_loop(0, 4, section, 0)
    send_levels(1, 0, CUT_F)

    for copy in loads[3:]:
        copy.wait()

    kx_all = lax.broadcasted_iota(jnp.int32, (HALF, 128), 0).astype(f32) * UNIT

    def into_modes(e):
        all_of(recv_x.at[e], big_recv.at[e])
        g = [recv_x[e, :, c * 8 : (c + 1) * 8, :].reshape(N, 128) for c in range(3)]
        high, low = split(jnp.concatenate(g, axis=1))
        modes = dot3(tab[0], tab[1], high, low)
        c0, s0 = modes[:HALF, :128], modes[HALF:, :128]
        uc = modes[:HALF, 256:] + kx_all * s0
        us = modes[HALF:, 256:] - kx_all * c0
        vc, vs = modes[:HALF, 128:256], modes[HALF:, 128:256]
        for j in range(4):
            for r, block in enumerate((uc, us, vc, vs)):
                grp[e, j, r * 64 : (r + 1) * 64, :] = block[j * 64 : (j + 1) * 64]
        swap(e, grp, grp_in, grp_send, grp_recv)

    rate = rates[level]

    def solve(e):
        all_of(grp_in.at[e], grp_recv.at[e])
        high, low = split(jnp.concatenate([grp_in[e, j] for j in range(4)], axis=1))
        spec = dot3(high, low, ttab[0], ttab[1])
        row = lax.broadcasted_iota(jnp.int32, (128, HALF), 0) % 64 + part * 64
        kx = row.astype(f32) * UNIT
        ky = lanes((128, HALF)).astype(f32) * UNIT
        factor = -1.0 / (rate + kx * kx + ky * ky)
        pc = factor * (spec[:128, :HALF] + ky * spec[128:, HALF:])
        ps = factor * (spec[:128, HALF:] - ky * spec[128:, :HALF])
        both = jnp.concatenate(
            [
                jnp.concatenate([pc, ps], axis=1),
                jnp.concatenate([ky * ps, -(ky * pc)], axis=1),
            ],
            axis=0,
        )
        high, low = split(both)
        out = dot3(high, low, tab[0], tab[1])
        for j in range(4):
            bck[e, j] = out[:, j * 128 : (j + 1) * 128]
        swap(e, bck, bck_in, bck_send, bck_recv)

    def from_modes(e):
        all_of(bck_in.at[e], bck_recv.at[e])
        r = [
            jnp.concatenate([bck_in[e, j, k * 64 : (k + 1) * 64, :] for j in range(4)], axis=0)
            for k in range(4)
        ]
        pc, ps, yc, ys = r
        rhs = jnp.concatenate(
            [
                jnp.concatenate([kx_all * ps, yc, pc], axis=1),
                jnp.concatenate([-(kx_all * pc), ys, ps], axis=1),
            ],
            axis=0,
        )
        high, low = split(rhs)
        out = dot3(ttab[0], ttab[1], high, low)
        for c in range(3):
            back_x[e, :, c * 8 : (c + 1) * 8, :] = out[:, c * 128 : (c + 1) * 128].reshape(64, 8, 128)

    into_modes(0)
    send_levels(1, CUT_F, 64)
    solve(0)
    into_modes(1)
    from_modes(0)
    send_columns(0, 0, CUT_R)
    solve(1)
    send_columns(0, CUT_R, 64)
    from_modes(1)
    send_columns(1)

    all_of(back_z.at[0], ret_recv.at[0])

    def levels_of(e, c, x):
        return jnp.concatenate(
            [
                back_z[e, pl.ds(c * 8 + x, 64, stride=24), :],
                back_z[e, pl.ds(c * 8 + x + 1, 64, stride=24), :],
            ],
            axis=1,
        )

    def adjoint_out(xp, carry):
        x = xp * 2
        total = [zero, zero]
        for c in range(3):
            g = apply(m4[6 if c == 2 else 5], levels_of(0, c, x))
            for k in range(2):
                v = cotv[c, x + k] + g[:, k * 128 : (k + 1) * 128]
                cotv[c, x + k] = v
                total[k] = total[k] + v * lap[c, x + k]
        for k in range(2):
            grad[x + k] = step_weight * profile * total[k]
        return carry

    lax.fori_loop(0, 4, adjoint_out, 0)
    outs = [
        pltpu.make_async_copy(cotv, o_adj, out_sem.at[0]),
        pltpu.make_async_copy(grad, o_grad, out_sem.at[1]),
        pltpu.make_async_copy(sec, o_new, out_sem.at[2]),
    ]
    outs[0].start()
    outs[1].start()

    all_of(back_z.at[1], ret_recv.at[1])

    def forward_out(xp, carry):
        x = xp * 2
        for c in range(3):
            g = apply(m4[8 if c == 2 else 7], levels_of(1, c, x))
            for k in range(2):
                sec[c, x + k] = sec[c, x + k] - g[:, k * 128 : (k + 1) * 128]
        return carry

    lax.fori_loop(0, 4, forward_out, 0)
    outs[2].start()

    for copy in halos:
        copy.wait_send()
    for e in range(2):

        @pl.when(q == part)
        def _():
            all_of(recv_x.at[e, pl.ds(0, 63)], big_send.at[e])
            all_of(recv_x.at[e, pl.ds(0, 63)], ret_send.at[e])

        @pl.when(q != part)
        def _():
            all_of(recv_x.at[e], big_send.at[e])
            all_of(recv_x.at[e], ret_send.at[e])

        all_of(grp.at[e, pl.ds(0, 3)], grp_send.at[e])
        all_of(bck.at[e, pl.ds(0, 3)], bck_send.at[e])
    for copy in outs:
        copy.wait()


def body(velocity, cotangent, coefficient, level_profile, vert_deriv, eigen_vectors, eigen_inverse, eigen_rates):
    squares = jnp.stack([vert_deriv, eigen_vectors, eigen_inverse])
    mats = jnp.tile(jnp.concatenate([squares, jnp.swapaxes(squares, 1, 2)], axis=0), (1, 1, 4))
    profile = jnp.broadcast_to(level_profile[:, None], (64, 128))
    tables = [jnp.asarray(t) for t in basis()]
    hbm = pl.BlockSpec(memory_space=pl.ANY)
    vmem = pl.BlockSpec(memory_space=pltpu.VMEM)
    smem = pl.BlockSpec(memory_space=pltpu.SMEM)
    field = (3, 8, 64, 128)
    dma = pltpu.SemaphoreType.DMA
    return pl.pallas_call(
        body_kernel,
        out_shape=(
            jax.ShapeDtypeStruct(field, f32),
            jax.ShapeDtypeStruct(field, f32),
            jax.ShapeDtypeStruct(field[1:], f32),
        ),
        in_specs=[hbm, hbm, hbm, vmem, vmem, smem, hbm, hbm, hbm, hbm],
        out_specs=(hbm, hbm, hbm),
        scratch_shapes=[
            pltpu.VMEM((3, 10, 64, 128), f32),
            pltpu.VMEM(field, f32),
            pltpu.VMEM(field[1:], f32),
            pltpu.VMEM(field, f32),
            pltpu.VMEM(field, f32),
            pltpu.VMEM(field[1:], f32),
            pltpu.VMEM((2, 64, 128), f32),
            pltpu.VMEM((2, 64, 128), f32),
            pltpu.VMEM((2, 1536, 128), f32),
            pltpu.VMEM((2, 64, 24, 128), f32),
            pltpu.VMEM((2, 64, 24, 128), f32),
            pltpu.VMEM((2, 1536, 128), f32),
            pltpu.VMEM((2, 4, 256, 128), f32),
            pltpu.VMEM((2, 4, 256, 128), f32),
            pltpu.VMEM((2, 4, 256, 128), f32),
            pltpu.VMEM((2, 4, 256, 128), f32),
            pltpu.VMEM((2, N, N), bf16),
            pltpu.VMEM((2, N, N), bf16),
            pltpu.VMEM((9, 64, 256), bf16),
            dma((7,)),
            dma((3,)),
            dma((2,)), dma((2,)), dma((2,)), dma((2,)),
            dma((2,)), dma((2,)), dma((2,)), dma((2,)),
            dma((2,)), dma((2,)), dma((2,)), dma((2,)),
        ],
        compiler_params=pltpu.CompilerParams(
            collective_id=0, has_side_effects=True, vmem_limit_bytes=56 << 20
        ),
        name="substep",
    )(velocity, cotangent, coefficient, profile, mats, eigen_rates, *tables)


def solution(mesh):
    field = P(None, "gx", None, "gy")
    cell = P("gx", None, "gy")
    in_specs = (field, field, cell, P(), P(), P(), P(), P())
    return jax.shard_map(body, mesh=mesh, in_specs=in_specs, out_specs=(field, field, cell), check_vma=False)
```

```python
import functools
import math

import jax
import jax.numpy as jnp
import ml_dtypes
import numpy as np
from jax import lax
from jax.experimental import pallas as pl
from jax.experimental.pallas import tpu as pltpu
from jax.sharding import PartitionSpec as P

MESH = pl.DeviceIdType.MESH
step_weight = 0.3 * 8.0 / 15.0
N = 512
CUT_F = 32
CUT_R = 32
HALF = N // 2
UNIT = 2.0 * math.pi / N
f32 = jnp.float32
bf16 = jnp.bfloat16


def basis():
    k = np.arange(HALF)[:, None]
    x = np.arange(N)[None, :]
    angle = (k * x % N) * (2.0 * np.pi / N)
    cos, sin = np.cos(angle), np.sin(angle)
    sin[0] = np.cos(np.pi * x[0])
    scale = np.full((HALF, 1), math.sqrt(2.0 / N))
    scale[0] = math.sqrt(1.0 / N)
    table = np.concatenate([scale * cos, scale * sin], axis=0)
    out = []
    for t in (table, table.T):
        high = t.astype(ml_dtypes.bfloat16)
        low = (t - high.astype(np.float64)).astype(ml_dtypes.bfloat16)
        out += [np.ascontiguousarray(high), np.ascontiguousarray(low)]
    return out


def split(v):
    high = v.astype(bf16)
    return high, (v - high.astype(f32)).astype(bf16)


def dot(a, b):
    return jnp.dot(a, b, preferred_element_type=f32)


def dot3(a_high, a_low, b_high, b_low):
    return dot(a_high, b_high) + (dot(a_high, b_low) + dot(a_low, b_high))


def lanes(shape):
    return lax.broadcasted_iota(jnp.int32, shape, len(shape) - 1)


def quad(m, flip=False):
    r = lax.broadcasted_iota(jnp.int32, (64, 256), 0)
    c = lanes((64, 256))
    high, low = split(m)
    dims = (((0 if flip else 1,), (0,)), ((), ()))
    out = 0.0
    for term, odd in ((high, 0), (low, 1)):
        pick = jnp.where((c % 64 == r) & ((c // 64) % 2 == odd), 1.0, 0.0).astype(bf16)
        out = out + lax.dot_general(term, pick, dims, preferred_element_type=f32)
    return out.astype(bf16)


def apply(m4, f):
    high, low = split(f)
    return dot(m4, jnp.concatenate([high, high, low, low], axis=0))


def body_kernel(
    vel, cot, coef, deriv, vectors, inverse, prof, rates, t_high, t_low, tt_high, tt_low,
    o_new, o_adj, o_grad,
    velp, cotv, coefv, lap, sec, grad, ycol, yhalo,
    send_z, recv_x, back_x, back_z, grp, grp_in, bck, bck_in,
    tab, ttab, mats, m4,
    load_sem, out_sem, hx_send, hx_recv, hy_send, hy_recv,
    big_send, big_recv, grp_send, grp_recv, bck_send, bck_recv, ret_send, ret_recv,
):
    gx = lax.axis_index("gx")
    q = lax.axis_index("gy")
    core = gx % 2
    cy = (gx // 2) % 4
    cx = gx // 16
    cz = ((gx // 8) % 2) * 4 + q
    part = ((cy + cz) % 2) * 2 + core
    level = (cx * 2 + cy // 2) * 8 + cz

    def gx_of(x, z, y, c):
        return ((x * 2 + z // 4) * 4 + y) * 2 + c

    def member(j):
        return (gx_of(cx, cz, (cy // 2) * 2 + (j // 2 + cz) % 2, j % 2), q)

    east, west = ((gx + 1) % 64, q), ((gx + 63) % 64, q)
    north, south = (gx, (q + 1) % 4), (gx, (q + 3) % 4)

    loads = [
        pltpu.make_async_copy(cot, cotv, load_sem.at[0]),
        pltpu.make_async_copy(vel, velp.at[:, pl.ds(1, 8)], load_sem.at[1]),
        pltpu.make_async_copy(coef, coefv, load_sem.at[2]),
        pltpu.make_async_copy(t_high, tab.at[0], load_sem.at[3]),
        pltpu.make_async_copy(t_low, tab.at[1], load_sem.at[4]),
        pltpu.make_async_copy(tt_high, ttab.at[0], load_sem.at[5]),
        pltpu.make_async_copy(tt_low, ttab.at[1], load_sem.at[6]),
        pltpu.make_async_copy(deriv, mats.at[0], load_sem.at[7]),
        pltpu.make_async_copy(vectors, mats.at[1], load_sem.at[8]),
        pltpu.make_async_copy(inverse, mats.at[2], load_sem.at[9]),
    ]
    for copy in loads:
        copy.start()

    barrier = pltpu.get_barrier_semaphore()

    def tell(dev):
        pl.semaphore_signal(barrier, inc=1, device_id=dev, device_id_type=MESH)

    def tell_source(t, carry):
        i = (gx + t) % 64

        @pl.when(jnp.logical_or(i != gx, q != part))
        def _():
            tell((i, part))

        return carry

    lax.fori_loop(0, 64, tell_source, 0)
    for d in range(1, 4):
        tell(member((part + d) % 4))
    for dev in (east, west, north, south):
        tell(dev)

    for copy in loads[7:]:
        copy.wait()
    D, V, E = mats[0], mats[1], mats[2]
    m4[2] = quad(D)
    DV = apply(m4[2], V)
    m4[0] = quad(-V, True)
    m4[1] = quad(DV, True)

    loads[0].wait()

    def adjoint_in(xp, carry):
        x = xp * 2
        for c in range(3):
            f = jnp.concatenate([cotv[c, x], cotv[c, x + 1]], axis=1)
            g = apply(m4[1 if c == 2 else 0], f)
            send_z[0, pl.ds(c * 8 + x, 64, stride=24), :] = g[:, :128]
            send_z[0, pl.ds(c * 8 + x + 1, 64, stride=24), :] = g[:, 128:]
        return carry

    lax.fori_loop(0, 4, adjoint_in, 0)

    loads[1].wait()
    lane = lanes((64, 128))

    def pack(x, carry):
        first, last = carry
        for c in range(3):
            f = velp[c, x + 1]
            j = c * 8 + x
            first = jnp.where(lane == j, pltpu.roll(f, j, 1), first)
            last = jnp.where(lane == j, pltpu.roll(f, j + 1, 1), last)
        return first, last

    zero = jnp.zeros((64, 128), f32)
    first, last = lax.fori_loop(0, 8, pack, (zero, zero))
    ycol[0] = first
    ycol[1] = last

    @pl.when(q == part)
    def _():
        pl.semaphore_wait(barrier, 70)

    @pl.when(q != part)
    def _():
        pl.semaphore_wait(barrier, 71)

    def remote(src, dst, ssem, rsem, dev):
        return pltpu.make_async_remote_copy(
            src_ref=src, dst_ref=dst, send_sem=ssem, recv_sem=rsem,
            device_id=dev, device_id_type=MESH,
        )

    halos = [
        remote(velp.at[:, 8], velp.at[:, 0], hx_send.at[0], hx_recv.at[0], east),
        remote(velp.at[:, 1], velp.at[:, 9], hx_send.at[1], hx_recv.at[1], west),
        remote(ycol.at[1], yhalo.at[0], hy_send.at[0], hy_recv.at[0], north),
        remote(ycol.at[0], yhalo.at[1], hy_send.at[1], hy_recv.at[1], south),
    ]
    for copy in halos:
        copy.start()

    def send_levels(e, start=0, stop=64):
        def go(t, carry):
            dz = t % 8
            u = (t // 8 + 2 * part) % 8
            off = (dz % 2) * (4 - (dz + 1) // 2) + (1 - dz % 2) * (4 + dz // 2)
            z = (cz + off) % 8
            x = (cx + u % 4) % 4
            h = (cy // 2 + u // 4) % 2
            target = gx_of(x, z, h * 2 + (q // 2 + z) % 2, q % 2)
            home = (x * 2 + h) * 8 + z
            src = send_z.at[e, pl.ds(pl.multiple_of(home * 24, 8), 24), :]
            dst = recv_x.at[e, gx]
            mine = jnp.logical_and(home == level, q == part)

            @pl.when(mine)
            def _():
                pltpu.make_async_copy(src, dst, big_recv.at[e]).start()

            @pl.when(jnp.logical_not(mine))
            def _():
                remote(src, dst, big_send.at[e], big_recv.at[e], (target, z % 4)).start()

            return carry

        lax.fori_loop(start, stop, go, 0)

    def send_columns(e, start=0, stop=64):
        def go(t, carry):
            u = (t + 8 * cz) % 64
            h = u % 2
            c = (core + (u // 2) % 2) % 2
            x = (cx + (u // 4) % 4) % 4
            y = (cy + u // 16) % 4
            i = gx_of(x, h * 4, y, c)
            src = back_x.at[e, i]
            dst = back_z.at[e, pl.ds(pl.multiple_of(level * 24, 8), 24), :]
            mine = jnp.logical_and(i == gx, q == part)

            @pl.when(mine)
            def _():
                pltpu.make_async_copy(src, dst, ret_recv.at[e]).start()

            @pl.when(jnp.logical_not(mine))
            def _():
                remote(src, dst, ret_send.at[e], ret_recv.at[e], (i, part)).start()

            return carry

        lax.fori_loop(start, stop, go, 0)

    def all_of(ref, sem):
        pltpu.make_async_copy(ref, ref, sem).wait()

    def swap(e, out, into, ssem, rsem):
        for d in range(1, 4):
            j = (part + d) % 4
            remote(out.at[e, j], into.at[e, part], ssem.at[e], rsem.at[e], member(j)).start()
        pltpu.make_async_copy(out.at[e, part], into.at[e, part], rsem.at[e]).start()

    send_levels(0)

    ED = apply(quad(E), D)
    m4[3] = quad(E)
    m4[4] = quad(ED)
    m4[5] = quad(E, True)
    m4[6] = quad(-ED, True)
    m4[7] = quad(V)
    m4[8] = quad(DV)
    diagonal = lax.broadcasted_iota(jnp.int32, (64, 64), 0) == lanes((64, 64))
    column = jnp.sum(jnp.where(diagonal, jnp.broadcast_to(prof[...], (64, 64)), 0.0), axis=1, keepdims=True)
    profile = jnp.broadcast_to(column, (64, 128))

    halos[0].wait_recv()
    halos[1].wait_recv()
    halos[2].wait_recv()
    halos[3].wait_recv()
    loads[2].wait()

    def section(xp, carry):
        pair = []
        for x in (xp * 2, xp * 2 + 1):
            here = [velp[c, x + 1] for c in range(3)]
            rows = []
            for c in range(3):
                f = here[c]
                e, w = velp[c, x + 2], velp[c, x]
                j = c * 8 + x
                n = jnp.where(lane == 127, pltpu.roll(yhalo[1], 127 - j, 1), pltpu.roll(f, 127, 1))
                s = jnp.where(lane == 0, pltpu.roll(yhalo[0], (128 - j) % 128, 1), pltpu.roll(f, 1, 1))
                laplace = e + w + n + s - 4.0 * f
                lap[c, x] = laplace
                move = here[0] * (0.5 * (e - w)) + here[1] * (0.5 * (n - s))
                rows.append(f + step_weight * (coefv[x] * profile * laplace - move))
            pair.append((here, rows))
        for c in range(3):
            f = jnp.concatenate([pair[0][0][c], pair[1][0][c]], axis=1)
            slope = apply(m4[2], f)
            s = []
            for k in range(2):
                here, rows = pair[k]
                v = rows[c] - step_weight * (here[2] * slope[:, k * 128 : (k + 1) * 128])
                sec[c, xp * 2 + k] = v
                s.append(v)
            g = apply(m4[4 if c == 2 else 3], jnp.concatenate(s, axis=1))
            send_z[1, pl.ds(c * 8 + xp * 2, 64, stride=24), :] = g[:, :128]
            send_z[1, pl.ds(c * 8 + xp * 2 + 1, 64, stride=24), :] = g[:, 128:]
        return carry

    lax.fori_loop(0, 4, section, 0)
    send_levels(1, 0, CUT_F)

    for copy in loads[3:7]:
        copy.wait()

    kx_all = lax.broadcasted_iota(jnp.int32, (HALF, 128), 0).astype(f32) * UNIT

    def into_modes(e):
        all_of(recv_x.at[e], big_recv.at[e])
        g = [recv_x[e, :, c * 8 : (c + 1) * 8, :].reshape(N, 128) for c in range(3)]
        high, low = split(jnp.concatenate(g, axis=1))
        modes = dot3(tab[0], tab[1], high, low)
        c0, s0 = modes[:HALF, :128], modes[HALF:, :128]
        uc = modes[:HALF, 256:] + kx_all * s0
        us = modes[HALF:, 256:] - kx_all * c0
        vc, vs = modes[:HALF, 128:256], modes[HALF:, 128:256]
        for j in range(4):
            for r, block in enumerate((uc, us, vc, vs)):
                grp[e, j, r * 64 : (r + 1) * 64, :] = block[j * 64 : (j + 1) * 64]
        swap(e, grp, grp_in, grp_send, grp_recv)

    rate = rates[level]

    def solve(e):
        all_of(grp_in.at[e], grp_recv.at[e])
        high, low = split(jnp.concatenate([grp_in[e, j] for j in range(4)], axis=1))
        spec = dot3(high, low, ttab[0], ttab[1])
        row = lax.broadcasted_iota(jnp.int32, (128, HALF), 0) % 64 + part * 64
        kx = row.astype(f32) * UNIT
        ky = lanes((128, HALF)).astype(f32) * UNIT
        factor = -1.0 / (rate + kx * kx + ky * ky)
        pc = factor * (spec[:128, :HALF] + ky * spec[128:, HALF:])
        ps = factor * (spec[:128, HALF:] - ky * spec[128:, :HALF])
        both = jnp.concatenate(
            [
                jnp.concatenate([pc, ps], axis=1),
                jnp.concatenate([ky * ps, -(ky * pc)], axis=1),
            ],
            axis=0,
        )
        high, low = split(both)
        out = dot3(high, low, tab[0], tab[1])
        for j in range(4):
            bck[e, j] = out[:, j * 128 : (j + 1) * 128]
        swap(e, bck, bck_in, bck_send, bck_recv)

    def from_modes(e):
        all_of(bck_in.at[e], bck_recv.at[e])
        r = [
            jnp.concatenate([bck_in[e, j, k * 64 : (k + 1) * 64, :] for j in range(4)], axis=0)
            for k in range(4)
        ]
        pc, ps, yc, ys = r
        rhs = jnp.concatenate(
            [
                jnp.concatenate([kx_all * ps, yc, pc], axis=1),
                jnp.concatenate([-(kx_all * pc), ys, ps], axis=1),
            ],
            axis=0,
        )
        high, low = split(rhs)
        out = dot3(ttab[0], ttab[1], high, low)
        for c in range(3):
            back_x[e, :, c * 8 : (c + 1) * 8, :] = out[:, c * 128 : (c + 1) * 128].reshape(64, 8, 128)

    into_modes(0)
    send_levels(1, CUT_F, 64)
    solve(0)
    into_modes(1)
    from_modes(0)
    send_columns(0, 0, CUT_R)
    solve(1)
    send_columns(0, CUT_R, 64)
    from_modes(1)
    send_columns(1)

    all_of(back_z.at[0], ret_recv.at[0])

    def levels_of(e, c, x):
        return jnp.concatenate(
            [
                back_z[e, pl.ds(c * 8 + x, 64, stride=24), :],
                back_z[e, pl.ds(c * 8 + x + 1, 64, stride=24), :],
            ],
            axis=1,
        )

    def adjoint_out(xp, carry):
        x = xp * 2
        total = [zero, zero]
        for c in range(3):
            g = apply(m4[6 if c == 2 else 5], levels_of(0, c, x))
            for k in range(2):
                v = cotv[c, x + k] + g[:, k * 128 : (k + 1) * 128]
                cotv[c, x + k] = v
                total[k] = total[k] + v * lap[c, x + k]
        for k in range(2):
            grad[x + k] = step_weight * profile * total[k]
        return carry

    lax.fori_loop(0, 4, adjoint_out, 0)
    outs = [
        pltpu.make_async_copy(cotv, o_adj, out_sem.at[0]),
        pltpu.make_async_copy(grad, o_grad, out_sem.at[1]),
        pltpu.make_async_copy(sec, o_new, out_sem.at[2]),
    ]
    outs[0].start()
    outs[1].start()

    all_of(back_z.at[1], ret_recv.at[1])

    def forward_out(xp, carry):
        x = xp * 2
        for c in range(3):
            g = apply(m4[8 if c == 2 else 7], levels_of(1, c, x))
            for k in range(2):
                sec[c, x + k] = sec[c, x + k] - g[:, k * 128 : (k + 1) * 128]
        return carry

    lax.fori_loop(0, 4, forward_out, 0)
    outs[2].start()

    for copy in halos:
        copy.wait_send()
    for e in range(2):

        @pl.when(q == part)
        def _():
            all_of(recv_x.at[e, pl.ds(0, 63)], big_send.at[e])
            all_of(recv_x.at[e, pl.ds(0, 63)], ret_send.at[e])

        @pl.when(q != part)
        def _():
            all_of(recv_x.at[e], big_send.at[e])
            all_of(recv_x.at[e], ret_send.at[e])

        all_of(grp.at[e, pl.ds(0, 3)], grp_send.at[e])
        all_of(bck.at[e, pl.ds(0, 3)], bck_send.at[e])
    for copy in outs:
        copy.wait()


def body(velocity, cotangent, coefficient, level_profile, vert_deriv, eigen_vectors, eigen_inverse, eigen_rates):
    tables = [jnp.asarray(t) for t in basis()]
    hbm = pl.BlockSpec(memory_space=pl.ANY)
    vmem = pl.BlockSpec(memory_space=pltpu.VMEM)
    smem = pl.BlockSpec(memory_space=pltpu.SMEM)
    field = (3, 8, 64, 128)
    dma = pltpu.SemaphoreType.DMA
    return pl.pallas_call(
        body_kernel,
        out_shape=(
            jax.ShapeDtypeStruct(field, f32),
            jax.ShapeDtypeStruct(field, f32),
            jax.ShapeDtypeStruct(field[1:], f32),
        ),
        in_specs=[hbm] * 6 + [vmem, smem] + [hbm] * 4,
        out_specs=(hbm, hbm, hbm),
        scratch_shapes=[
            pltpu.VMEM((3, 10, 64, 128), f32),
            pltpu.VMEM(field, f32),
            pltpu.VMEM(field[1:], f32),
            pltpu.VMEM(field, f32),
            pltpu.VMEM(field, f32),
            pltpu.VMEM(field[1:], f32),
            pltpu.VMEM((2, 64, 128), f32),
            pltpu.VMEM((2, 64, 128), f32),
            pltpu.VMEM((2, 1536, 128), f32),
            pltpu.VMEM((2, 64, 24, 128), f32),
            pltpu.VMEM((2, 64, 24, 128), f32),
            pltpu.VMEM((2, 1536, 128), f32),
            pltpu.VMEM((2, 4, 256, 128), f32),
            pltpu.VMEM((2, 4, 256, 128), f32),
            pltpu.VMEM((2, 4, 256, 128), f32),
            pltpu.VMEM((2, 4, 256, 128), f32),
            pltpu.VMEM((2, N, N), bf16),
            pltpu.VMEM((2, N, N), bf16),
            pltpu.VMEM((3, 64, 64), f32),
            pltpu.VMEM((9, 64, 256), bf16),
            dma((10,)),
            dma((3,)),
            dma((2,)), dma((2,)), dma((2,)), dma((2,)),
            dma((2,)), dma((2,)), dma((2,)), dma((2,)),
            dma((2,)), dma((2,)), dma((2,)), dma((2,)),
        ],
        compiler_params=pltpu.CompilerParams(
            collective_id=0, has_side_effects=True, vmem_limit_bytes=56 << 20
        ),
        name="substep",
    )(
        velocity, cotangent, coefficient, vert_deriv, eigen_vectors, eigen_inverse,
        level_profile[None, :], eigen_rates, *tables,
    )


def solution(mesh):
    field = P(None, "gx", None, "gy")
    cell = P("gx", None, "gy")
    in_specs = (field, field, cell, P(), P(), P(), P(), P())
    return jax.shard_map(body, mesh=mesh, in_specs=in_specs, out_specs=(field, field, cell), check_vma=False)
```

```python
import functools
import math

import jax
import jax.numpy as jnp
import ml_dtypes
import numpy as np
from jax import lax
from jax.experimental import pallas as pl
from jax.experimental.pallas import tpu as pltpu
from jax.sharding import PartitionSpec as P

MESH = pl.DeviceIdType.MESH
step_weight = 0.3 * 8.0 / 15.0
N = 512
CUT_F = 32
CUT_R = 32
HALF = N // 2
UNIT = 2.0 * math.pi / N
f32 = jnp.float32
bf16 = jnp.bfloat16


def basis():
    k = np.arange(HALF)[:, None]
    x = np.arange(N)[None, :]
    angle = (k * x % N) * (2.0 * np.pi / N)
    cos, sin = np.cos(angle), np.sin(angle)
    sin[0] = np.cos(np.pi * x[0])
    scale = np.full((HALF, 1), math.sqrt(2.0 / N))
    scale[0] = math.sqrt(1.0 / N)
    table = np.concatenate([scale * cos, scale * sin], axis=0)
    out = []
    for t in (table, table.T):
        high = t.astype(ml_dtypes.bfloat16)
        low = (t - high.astype(np.float64)).astype(ml_dtypes.bfloat16)
        out += [np.ascontiguousarray(high), np.ascontiguousarray(low)]
    return out


def split(v):
    high = v.astype(bf16)
    return high, (v - high.astype(f32)).astype(bf16)


def dot(a, b):
    return jnp.dot(a, b, preferred_element_type=f32)


def dot3(a_high, a_low, b_high, b_low):
    return dot(a_high, b_high) + (dot(a_high, b_low) + dot(a_low, b_high))


def lanes(shape):
    return lax.broadcasted_iota(jnp.int32, shape, len(shape) - 1)


def quad(m, flip=False):
    r = lax.broadcasted_iota(jnp.int32, (64, 256), 0)
    c = lanes((64, 256))
    high, low = split(m)
    dims = (((0 if flip else 1,), (0,)), ((), ()))
    out = 0.0
    for term, odd in ((high, 0), (low, 1)):
        pick = jnp.where((c % 64 == r) & ((c // 64) % 2 == odd), 1.0, 0.0).astype(bf16)
        out = out + lax.dot_general(term, pick, dims, preferred_element_type=f32)
    return out.astype(bf16)


def apply(m4, f):
    high, low = split(f)
    return dot(m4, jnp.concatenate([high, high, low, low], axis=0))


def body_kernel(
    vel, cot, coef, deriv, vectors, inverse, prof, rates, t_high, t_low, tt_high, tt_low,
    o_new, o_adj, o_grad,
    velp, cotv, coefv, lap, sec, grad, ycol, yhalo,
    send_z, recv_x, back_x, back_z, grp, grp_in, bck, bck_in,
    tab, ttab, mats, m4,
    load_sem, out_sem, hx_send, hx_recv, hy_send, hy_recv,
    big_send, big_recv, grp_send, grp_recv, bck_send, bck_recv, ret_send, ret_recv,
):
    gx = lax.axis_index("gx")
    q = lax.axis_index("gy")
    core = gx % 2
    cy = (gx // 2) % 4
    cx = gx // 16
    cz = ((gx // 8) % 2) * 4 + q
    part = ((cy + cz) % 2) * 2 + core
    level = (cx * 2 + cy // 2) * 8 + cz

    def gx_of(x, z, y, c):
        return ((x * 2 + z // 4) * 4 + y) * 2 + c

    def member(j):
        return (gx_of(cx, cz, (cy // 2) * 2 + (j // 2 + cz) % 2, j % 2), q)

    east, west = ((gx + 1) % 64, q), ((gx + 63) % 64, q)
    north, south = (gx, (q + 1) % 4), (gx, (q + 3) % 4)

    loads = [
        pltpu.make_async_copy(cot, cotv, load_sem.at[0]),
        pltpu.make_async_copy(vel, velp.at[:, pl.ds(1, 8)], load_sem.at[1]),
        pltpu.make_async_copy(coef, coefv, load_sem.at[2]),
        pltpu.make_async_copy(t_high, tab.at[0], load_sem.at[3]),
        pltpu.make_async_copy(t_low, tab.at[1], load_sem.at[4]),
        pltpu.make_async_copy(tt_high, ttab.at[0], load_sem.at[5]),
        pltpu.make_async_copy(tt_low, ttab.at[1], load_sem.at[6]),
        pltpu.make_async_copy(deriv, mats.at[0], load_sem.at[7]),
        pltpu.make_async_copy(vectors, mats.at[1], load_sem.at[8]),
        pltpu.make_async_copy(inverse, mats.at[2], load_sem.at[9]),
    ]
    for copy in loads:
        copy.start()

    barrier = pltpu.get_barrier_semaphore()

    def tell(dev):
        pl.semaphore_signal(barrier, inc=1, device_id=dev, device_id_type=MESH)

    def tell_source(t, carry):
        i = (gx + t) % 64

        @pl.when(jnp.logical_or(i != gx, q != part))
        def _():
            tell((i, part))

        return carry

    lax.fori_loop(0, 64, tell_source, 0)
    for d in range(1, 4):
        tell(member((part + d) % 4))
    for dev in (east, west, north, south):
        tell(dev)

    for copy in loads[7:]:
        copy.wait()
    D, V, E = mats[0], mats[1], mats[2]
    m4[2] = quad(D)
    DV = apply(m4[2], V)
    m4[0] = quad(-V, True)
    m4[1] = quad(DV, True)

    loads[0].wait()

    def adjoint_in(xp, carry):
        x = xp * 2
        for c in range(3):
            f = jnp.concatenate([cotv[c, x], cotv[c, x + 1]], axis=1)
            g = apply(m4[1 if c == 2 else 0], f)
            send_z[0, pl.ds(c * 8 + x, 64, stride=24), :] = g[:, :128]
            send_z[0, pl.ds(c * 8 + x + 1, 64, stride=24), :] = g[:, 128:]
        return carry

    lax.fori_loop(0, 4, adjoint_in, 0)

    loads[1].wait()
    lane = lanes((64, 128))

    def pack(x, carry):
        first, last = carry
        for c in range(3):
            f = velp[c, x + 1]
            j = c * 8 + x
            first = jnp.where(lane == j, pltpu.roll(f, j, 1), first)
            last = jnp.where(lane == j, pltpu.roll(f, j + 1, 1), last)
        return first, last

    zero = jnp.zeros((64, 128), f32)
    first, last = lax.fori_loop(0, 8, pack, (zero, zero))
    ycol[0] = first
    ycol[1] = last

    @pl.when(q == part)
    def _():
        pl.semaphore_wait(barrier, 70)

    @pl.when(q != part)
    def _():
        pl.semaphore_wait(barrier, 71)

    def remote(src, dst, ssem, rsem, dev):
        return pltpu.make_async_remote_copy(
            src_ref=src, dst_ref=dst, send_sem=ssem, recv_sem=rsem,
            device_id=dev, device_id_type=MESH,
        )

    halos = [
        remote(velp.at[:, 8], velp.at[:, 0], hx_send.at[0], hx_recv.at[0], east),
        remote(velp.at[:, 1], velp.at[:, 9], hx_send.at[1], hx_recv.at[1], west),
        remote(ycol.at[1], yhalo.at[0], hy_send.at[0], hy_recv.at[0], north),
        remote(ycol.at[0], yhalo.at[1], hy_send.at[1], hy_recv.at[1], south),
    ]
    for copy in halos:
        copy.start()

    def send_levels(e, start=0, stop=64):
        def go(t, carry):
            dz = t % 8
            u = (t // 8 + 2 * part) % 8
            off = (dz % 2) * (4 - (dz + 1) // 2) + (1 - dz % 2) * (4 + dz // 2)
            z = (cz + off) % 8
            x = (cx + u % 4) % 4
            h = (cy // 2 + u // 4) % 2
            target = gx_of(x, z, h * 2 + (q // 2 + z) % 2, q % 2)
            home = (x * 2 + h) * 8 + z
            src = send_z.at[e, pl.ds(pl.multiple_of(home * 24, 8), 24), :]
            dst = recv_x.at[e, gx]
            mine = jnp.logical_and(home == level, q == part)

            @pl.when(mine)
            def _():
                pltpu.make_async_copy(src, dst, big_recv.at[e]).start()

            @pl.when(jnp.logical_not(mine))
            def _():
                remote(src, dst, big_send.at[e], big_recv.at[e], (target, z % 4)).start()

            return carry

        lax.fori_loop(start, stop, go, 0)

    def send_columns(e, start=0, stop=64):
        def go(t, carry):
            u = (t + 8 * cz) % 64
            h = u % 2
            c = (core + (u // 2) % 2) % 2
            x = (cx + (u // 4) % 4) % 4
            y = (cy + u // 16) % 4
            i = gx_of(x, h * 4, y, c)
            src = back_x.at[e, i]
            dst = back_z.at[e, pl.ds(pl.multiple_of(level * 24, 8), 24), :]
            mine = jnp.logical_and(i == gx, q == part)

            @pl.when(mine)
            def _():
                pltpu.make_async_copy(src, dst, ret_recv.at[e]).start()

            @pl.when(jnp.logical_not(mine))
            def _():
                remote(src, dst, ret_send.at[e], ret_recv.at[e], (i, part)).start()

            return carry

        lax.fori_loop(start, stop, go, 0)

    def all_of(ref, sem):
        pltpu.make_async_copy(ref, ref, sem).wait()

    def swap(e, out, into, ssem, rsem):
        for d in range(1, 4):
            j = (part + d) % 4
            remote(out.at[e, j], into.at[e, part], ssem.at[e], rsem.at[e], member(j)).start()
        pltpu.make_async_copy(out.at[e, part], into.at[e, part], rsem.at[e]).start()

    send_levels(0)

    ED = apply(quad(E), D)
    m4[3] = quad(E)
    m4[4] = quad(ED)
    m4[5] = quad(E, True)
    m4[6] = quad(-ED, True)
    m4[7] = quad(V)
    m4[8] = quad(DV)
    diagonal = lax.broadcasted_iota(jnp.int32, (64, 64), 0) == lanes((64, 64))
    column = jnp.sum(jnp.where(diagonal, jnp.broadcast_to(prof[...], (64, 64)), 0.0), axis=1, keepdims=True)
    profile = jnp.broadcast_to(column, (64, 128))

    halos[0].wait_recv()
    halos[1].wait_recv()
    halos[2].wait_recv()
    halos[3].wait_recv()
    loads[2].wait()

    def section(xp, carry):
        pair = []
        for x in (xp * 2, xp * 2 + 1):
            here = [velp[c, x + 1] for c in range(3)]
            rows = []
            for c in range(3):
                f = here[c]
                e, w = velp[c, x + 2], velp[c, x]
                j = c * 8 + x
                n = jnp.where(lane == 127, pltpu.roll(yhalo[1], 127 - j, 1), pltpu.roll(f, 127, 1))
                s = jnp.where(lane == 0, pltpu.roll(yhalo[0], (128 - j) % 128, 1), pltpu.roll(f, 1, 1))
                laplace = e + w + n + s - 4.0 * f
                lap[c, x] = laplace
                move = here[0] * (0.5 * (e - w)) + here[1] * (0.5 * (n - s))
                rows.append(f + step_weight * (coefv[x] * profile * laplace - move))
            pair.append((here, rows))
        for c in range(3):
            f = jnp.concatenate([pair[0][0][c], pair[1][0][c]], axis=1)
            slope = apply(m4[2], f)
            s = []
            for k in range(2):
                here, rows = pair[k]
                v = rows[c] - step_weight * (here[2] * slope[:, k * 128 : (k + 1) * 128])
                sec[c, xp * 2 + k] = v
                s.append(v)
            g = apply(m4[4 if c == 2 else 3], jnp.concatenate(s, axis=1))
            send_z[1, pl.ds(c * 8 + xp * 2, 64, stride=24), :] = g[:, :128]
            send_z[1, pl.ds(c * 8 + xp * 2 + 1, 64, stride=24), :] = g[:, 128:]
        return carry

    lax.fori_loop(0, 4, section, 0)
    send_levels(1, 0, CUT_F)

    for copy in loads[3:7]:
        copy.wait()

    kx_all = lax.broadcasted_iota(jnp.int32, (HALF, 128), 0).astype(f32) * UNIT

    def into_modes(e):
        all_of(recv_x.at[e], big_recv.at[e])
        g = [recv_x[e, :, c * 8 : (c + 1) * 8, :].reshape(N, 128) for c in range(3)]
        high, low = split(jnp.concatenate(g, axis=1))
        modes = dot3(tab[0], tab[1], high, low)
        c0, s0 = modes[:HALF, :128], modes[HALF:, :128]
        uc = modes[:HALF, 256:] + kx_all * s0
        us = modes[HALF:, 256:] - kx_all * c0
        vc, vs = modes[:HALF, 128:256], modes[HALF:, 128:256]
        for j in range(4):
            for r, block in enumerate((uc, us, vc, vs)):
                grp[e, j, r * 64 : (r + 1) * 64, :] = block[j * 64 : (j + 1) * 64]
        swap(e, grp, grp_in, grp_send, grp_recv)

    rate = rates[level]

    def solve(e):
        all_of(grp_in.at[e], grp_recv.at[e])
        high, low = split(jnp.concatenate([grp_in[e, j] for j in range(4)], axis=1))
        spec = dot3(high, low, ttab[0], ttab[1])
        row = lax.broadcasted_iota(jnp.int32, (128, HALF), 0) % 64 + part * 64
        kx = row.astype(f32) * UNIT
        ky = lanes((128, HALF)).astype(f32) * UNIT
        factor = -1.0 / (rate + kx * kx + ky * ky)
        pc = factor * (spec[:128, :HALF] + ky * spec[128:, HALF:])
        ps = factor * (spec[:128, HALF:] - ky * spec[128:, :HALF])
        both = jnp.concatenate(
            [
                jnp.concatenate([pc, ps], axis=1),
                jnp.concatenate([ky * ps, -(ky * pc)], axis=1),
            ],
            axis=0,
        )
        high, low = split(both)
        out = dot3(high, low, tab[0], tab[1])
        for j in range(4):
            bck[e, j] = out[:, j * 128 : (j + 1) * 128]
        swap(e, bck, bck_in, bck_send, bck_recv)

    def from_modes(e):
        all_of(bck_in.at[e], bck_recv.at[e])
        r = [
            jnp.concatenate([bck_in[e, j, k * 64 : (k + 1) * 64, :] for j in range(4)], axis=0)
            for k in range(4)
        ]
        pc, ps, yc, ys = r
        rhs = jnp.concatenate(
            [
                jnp.concatenate([kx_all * ps, yc, pc], axis=1),
                jnp.concatenate([-(kx_all * pc), ys, ps], axis=1),
            ],
            axis=0,
        )
        high, low = split(rhs)
        out = dot3(ttab[0], ttab[1], high, low)
        for c in range(3):
            back_x[e, :, c * 8 : (c + 1) * 8, :] = out[:, c * 128 : (c + 1) * 128].reshape(64, 8, 128)

    into_modes(0)
    send_levels(1, CUT_F, 64)
    solve(0)
    into_modes(1)
    from_modes(0)
    send_columns(0, 0, CUT_R)
    solve(1)
    send_columns(0, CUT_R, 64)
    from_modes(1)
    send_columns(1)

    all_of(back_z.at[0], ret_recv.at[0])

    def levels_of(e, c, x):
        return jnp.concatenate(
            [
                back_z[e, pl.ds(c * 8 + x, 64, stride=24), :],
                back_z[e, pl.ds(c * 8 + x + 1, 64, stride=24), :],
            ],
            axis=1,
        )

    def adjoint_out(xp, carry):
        x = xp * 2
        total = [zero, zero]
        for c in range(3):
            g = apply(m4[6 if c == 2 else 5], levels_of(0, c, x))
            for k in range(2):
                v = cotv[c, x + k] + g[:, k * 128 : (k + 1) * 128]
                cotv[c, x + k] = v
                total[k] = total[k] + v * lap[c, x + k]
        for k in range(2):
            grad[x + k] = step_weight * profile * total[k]
        return carry

    lax.fori_loop(0, 4, adjoint_out, 0)
    outs = [
        pltpu.make_async_copy(cotv, o_adj, out_sem.at[0]),
        pltpu.make_async_copy(grad, o_grad, out_sem.at[1]),
        pltpu.make_async_copy(sec, o_new, out_sem.at[2]),
    ]
    outs[0].start()
    outs[1].start()

    all_of(back_z.at[1], ret_recv.at[1])

    def forward_out(xp, carry):
        x = xp * 2
        for c in range(3):
            g = apply(m4[8 if c == 2 else 7], levels_of(1, c, x))
            for k in range(2):
                sec[c, x + k] = sec[c, x + k] - g[:, k * 128 : (k + 1) * 128]
        return carry

    lax.fori_loop(0, 4, forward_out, 0)
    outs[2].start()

    for copy in halos:
        copy.wait_send()
    for e in range(2):

        @pl.when(q == part)
        def _():
            all_of(recv_x.at[e, pl.ds(0, 63)], big_send.at[e])
            all_of(recv_x.at[e, pl.ds(0, 63)], ret_send.at[e])

        @pl.when(q != part)
        def _():
            all_of(recv_x.at[e], big_send.at[e])
            all_of(recv_x.at[e], ret_send.at[e])

        all_of(grp.at[e, pl.ds(0, 3)], grp_send.at[e])
        all_of(bck.at[e, pl.ds(0, 3)], bck_send.at[e])
    for copy in outs:
        copy.wait()


def place_kernel(a, b, c, to_a, to_b, to_c, va, vb, vc, sems):
    pieces = []
    for i in range(3):
        pieces.append((a.at[i], va.at[i], to_a.at[i]))
        pieces.append((b.at[i], vb.at[i], to_b.at[i]))
    pieces.append((c, vc, to_c))
    reads = [pltpu.make_async_copy(p[0], p[1], sems.at[0, i]) for i, p in enumerate(pieces)]
    writes = [pltpu.make_async_copy(p[1], p[2], sems.at[1, i]) for i, p in enumerate(pieces)]
    for copy in reads:
        copy.start()
    for read, write in zip(reads, writes):
        read.wait()
        write.start()
    for copy in writes:
        copy.wait()


def body(velocity, cotangent, coefficient, level_profile, vert_deriv, eigen_vectors, eigen_inverse, eigen_rates):
    tables = [jnp.asarray(t) for t in basis()]
    hbm = pl.BlockSpec(memory_space=pl.ANY)
    vmem = pl.BlockSpec(memory_space=pltpu.VMEM)
    smem = pl.BlockSpec(memory_space=pltpu.SMEM)
    field = (3, 8, 64, 128)
    dma = pltpu.SemaphoreType.DMA
    shapes = (
        jax.ShapeDtypeStruct(field, f32),
        jax.ShapeDtypeStruct(field, f32),
        jax.ShapeDtypeStruct(field[1:], f32),
    )
    results = pl.pallas_call(
        body_kernel,
        out_shape=shapes,
        in_specs=[hbm] * 6 + [vmem, smem] + [hbm] * 4,
        out_specs=(hbm, hbm, hbm),
        scratch_shapes=[
            pltpu.VMEM((3, 10, 64, 128), f32),
            pltpu.VMEM(field, f32),
            pltpu.VMEM(field[1:], f32),
            pltpu.VMEM(field, f32),
            pltpu.VMEM(field, f32),
            pltpu.VMEM(field[1:], f32),
            pltpu.VMEM((2, 64, 128), f32),
            pltpu.VMEM((2, 64, 128), f32),
            pltpu.VMEM((2, 1536, 128), f32),
            pltpu.VMEM((2, 64, 24, 128), f32),
            pltpu.VMEM((2, 64, 24, 128), f32),
            pltpu.VMEM((2, 1536, 128), f32),
            pltpu.VMEM((2, 4, 256, 128), f32),
            pltpu.VMEM((2, 4, 256, 128), f32),
            pltpu.VMEM((2, 4, 256, 128), f32),
            pltpu.VMEM((2, 4, 256, 128), f32),
            pltpu.VMEM((2, N, N), bf16),
            pltpu.VMEM((2, N, N), bf16),
            pltpu.VMEM((3, 64, 64), f32),
            pltpu.VMEM((9, 64, 256), bf16),
            dma((10,)),
            dma((3,)),
            dma((2,)), dma((2,)), dma((2,)), dma((2,)),
            dma((2,)), dma((2,)), dma((2,)), dma((2,)),
            dma((2,)), dma((2,)), dma((2,)), dma((2,)),
        ],
        compiler_params=pltpu.CompilerParams(
            collective_id=0, has_side_effects=True, vmem_limit_bytes=56 << 20
        ),
        name="substep",
    )(
        velocity, cotangent, coefficient, vert_deriv, eigen_vectors, eigen_inverse,
        level_profile[None, :], eigen_rates, *tables,
    )
    return pl.pallas_call(
        place_kernel,
        out_shape=shapes,
        in_specs=[hbm] * 3,
        out_specs=(hbm, hbm, hbm),
        scratch_shapes=[pltpu.VMEM(shape.shape, f32) for shape in shapes] + [dma((2, 7))],
        compiler_params=pltpu.CompilerParams(vmem_limit_bytes=56 << 20),
        name="place",
    )(*results)


def solution(mesh):
    field = P(None, "gx", None, "gy")
    cell = P("gx", None, "gy")
    in_specs = (field, field, cell, P(), P(), P(), P(), P())
    return jax.shard_map(body, mesh=mesh, in_specs=in_specs, out_specs=(field, field, cell), check_vma=False)
```

```python
import functools
import math

import jax
import jax.numpy as jnp
import ml_dtypes
import numpy as np
from jax import lax
from jax.experimental import pallas as pl
from jax.experimental.pallas import tpu as pltpu
from jax.sharding import PartitionSpec as P

MESH = pl.DeviceIdType.MESH
step_weight = 0.3 * 8.0 / 15.0
N = 512
CUT_F = 32
CUT_R = 32
HALF = N // 2
UNIT = 2.0 * math.pi / N
f32 = jnp.float32
bf16 = jnp.bfloat16


def basis():
    k = np.arange(HALF)[:, None]
    x = np.arange(N)[None, :]
    angle = (k * x % N) * (2.0 * np.pi / N)
    cos, sin = np.cos(angle), np.sin(angle)
    sin[0] = np.cos(np.pi * x[0])
    scale = np.full((HALF, 1), math.sqrt(2.0 / N))
    scale[0] = math.sqrt(1.0 / N)
    table = np.concatenate([scale * cos, scale * sin], axis=0)
    out = []
    for t in (table, table.T):
        high = t.astype(ml_dtypes.bfloat16)
        low = (t - high.astype(np.float64)).astype(ml_dtypes.bfloat16)
        out += [np.ascontiguousarray(high), np.ascontiguousarray(low)]
    return out


def split(v):
    high = v.astype(bf16)
    return high, (v - high.astype(f32)).astype(bf16)


def dot(a, b):
    return jnp.dot(a, b, preferred_element_type=f32)


def dot3(a_high, a_low, b_high, b_low):
    return dot(a_high, b_high) + (dot(a_high, b_low) + dot(a_low, b_high))


def lanes(shape):
    return lax.broadcasted_iota(jnp.int32, shape, len(shape) - 1)


def quad(m, flip=False):
    r = lax.broadcasted_iota(jnp.int32, (64, 256), 0)
    c = lanes((64, 256))
    high, low = split(m)
    dims = (((0 if flip else 1,), (0,)), ((), ()))
    out = 0.0
    for term, odd in ((high, 0), (low, 1)):
        pick = jnp.where((c % 64 == r) & ((c // 64) % 2 == odd), 1.0, 0.0).astype(bf16)
        out = out + lax.dot_general(term, pick, dims, preferred_element_type=f32)
    return out.astype(bf16)


def apply(m4, f):
    high, low = split(f)
    return dot(m4, jnp.concatenate([high, high, low, low], axis=0))


def body_kernel(
    vel, cot, coef, deriv, vectors, inverse, prof, rates, t_high, t_low, tt_high, tt_low,
    o_new, o_adj, o_grad,
    velp, cotv, coefv, lap, sec, grad, ycol, yhalo,
    send_z, recv_x, back_x, back_z, grp, grp_in, bck, bck_in,
    tab, ttab, mats, m4,
    load_sem, out_sem, hx_send, hx_recv, hy_send, hy_recv,
    big_send, big_recv, grp_send, grp_recv, bck_send, bck_recv, ret_send, ret_recv,
):
    gx = lax.axis_index("gx")
    q = lax.axis_index("gy")
    core = gx % 2
    cy = (gx // 2) % 4
    cx = gx // 16
    cz = ((gx // 8) % 2) * 4 + q
    part = ((cy + cz) % 2) * 2 + core
    level = (cx * 2 + cy // 2) * 8 + cz

    def gx_of(x, z, y, c):
        return ((x * 2 + z // 4) * 4 + y) * 2 + c

    def member(j):
        return (gx_of(cx, cz, (cy // 2) * 2 + (j // 2 + cz) % 2, j % 2), q)

    east, west = ((gx + 1) % 64, q), ((gx + 63) % 64, q)
    north, south = (gx, (q + 1) % 4), (gx, (q + 3) % 4)

    loads = [
        pltpu.make_async_copy(cot, cotv, load_sem.at[0]),
        pltpu.make_async_copy(vel, velp.at[:, pl.ds(1, 8)], load_sem.at[1]),
        pltpu.make_async_copy(coef, coefv, load_sem.at[2]),
        pltpu.make_async_copy(t_high, tab.at[0], load_sem.at[3]),
        pltpu.make_async_copy(t_low, tab.at[1], load_sem.at[4]),
        pltpu.make_async_copy(tt_high, ttab.at[0], load_sem.at[5]),
        pltpu.make_async_copy(tt_low, ttab.at[1], load_sem.at[6]),
        pltpu.make_async_copy(deriv, mats.at[0], load_sem.at[7]),
        pltpu.make_async_copy(vectors, mats.at[1], load_sem.at[8]),
        pltpu.make_async_copy(inverse, mats.at[2], load_sem.at[9]),
    ]
    for copy in loads:
        copy.start()

    barrier = pltpu.get_barrier_semaphore()

    def tell(dev):
        pl.semaphore_signal(barrier, inc=1, device_id=dev, device_id_type=MESH)

    def tell_source(t, carry):
        i = (gx + t) % 64

        @pl.when(jnp.logical_or(i != gx, q != part))
        def _():
            tell((i, part))

        return carry

    lax.fori_loop(0, 64, tell_source, 0)
    for d in range(1, 4):
        tell(member((part + d) % 4))
    for dev in (east, west, north, south):
        tell(dev)

    for copy in loads[7:]:
        copy.wait()
    D, V, E = mats[0], mats[1], mats[2]
    m4[2] = quad(D)
    DV = apply(m4[2], V)
    m4[0] = quad(-V, True)
    m4[1] = quad(DV, True)

    loads[0].wait()

    def adjoint_in(xp, carry):
        x = xp * 2
        for c in range(3):
            f = jnp.concatenate([cotv[c, x], cotv[c, x + 1]], axis=1)
            g = apply(m4[1 if c == 2 else 0], f)
            send_z[0, pl.ds(c * 8 + x, 64, stride=24), :] = g[:, :128]
            send_z[0, pl.ds(c * 8 + x + 1, 64, stride=24), :] = g[:, 128:]
        return carry

    lax.fori_loop(0, 4, adjoint_in, 0)

    loads[1].wait()
    lane = lanes((64, 128))

    def pack(x, carry):
        first, last = carry
        for c in range(3):
            f = velp[c, x + 1]
            j = c * 8 + x
            first = jnp.where(lane == j, pltpu.roll(f, j, 1), first)
            last = jnp.where(lane == j, pltpu.roll(f, j + 1, 1), last)
        return first, last

    zero = jnp.zeros((64, 128), f32)
    first, last = lax.fori_loop(0, 8, pack, (zero, zero))
    ycol[0] = first
    ycol[1] = last

    @pl.when(q == part)
    def _():
        pl.semaphore_wait(barrier, 70)

    @pl.when(q != part)
    def _():
        pl.semaphore_wait(barrier, 71)

    def remote(src, dst, ssem, rsem, dev):
        return pltpu.make_async_remote_copy(
            src_ref=src, dst_ref=dst, send_sem=ssem, recv_sem=rsem,
            device_id=dev, device_id_type=MESH,
        )

    halos = [
        remote(velp.at[:, 8], velp.at[:, 0], hx_send.at[0], hx_recv.at[0], east),
        remote(velp.at[:, 1], velp.at[:, 9], hx_send.at[1], hx_recv.at[1], west),
        remote(ycol.at[1], yhalo.at[0], hy_send.at[0], hy_recv.at[0], north),
        remote(ycol.at[0], yhalo.at[1], hy_send.at[1], hy_recv.at[1], south),
    ]
    for copy in halos:
        copy.start()

    def send_levels(e, start=0, stop=64):
        def go(t, carry):
            dz = t % 8
            u = (t // 8 + 2 * part) % 8
            off = (dz % 2) * (4 - (dz + 1) // 2) + (1 - dz % 2) * (4 + dz // 2)
            z = (cz + off) % 8
            x = (cx + u % 4) % 4
            h = (cy // 2 + u // 4) % 2
            target = gx_of(x, z, h * 2 + (q // 2 + z) % 2, q % 2)
            home = (x * 2 + h) * 8 + z
            src = send_z.at[e, pl.ds(pl.multiple_of(home * 24, 8), 24), :]
            dst = recv_x.at[e, gx]
            mine = jnp.logical_and(home == level, q == part)

            @pl.when(mine)
            def _():
                pltpu.make_async_copy(src, dst, big_recv.at[e]).start()

            @pl.when(jnp.logical_not(mine))
            def _():
                remote(src, dst, big_send.at[e], big_recv.at[e], (target, z % 4)).start()

            return carry

        lax.fori_loop(start, stop, go, 0)

    def send_columns(e, start=0, stop=64):
        def go(t, carry):
            u = (t + 8 * cz) % 64
            h = u % 2
            c = (core + (u // 2) % 2) % 2
            x = (cx + (u // 4) % 4) % 4
            y = (cy + u // 16) % 4
            i = gx_of(x, h * 4, y, c)
            src = back_x.at[e, i]
            dst = back_z.at[e, pl.ds(pl.multiple_of(level * 24, 8), 24), :]
            mine = jnp.logical_and(i == gx, q == part)

            @pl.when(mine)
            def _():
                pltpu.make_async_copy(src, dst, ret_recv.at[e]).start()

            @pl.when(jnp.logical_not(mine))
            def _():
                remote(src, dst, ret_send.at[e], ret_recv.at[e], (i, part)).start()

            return carry

        lax.fori_loop(start, stop, go, 0)

    def all_of(ref, sem):
        pltpu.make_async_copy(ref, ref, sem).wait()

    def swap(e, out, into, ssem, rsem):
        for d in (2, 1, 3):
            j = (part + d) % 4
            remote(out.at[e, j], into.at[e, part], ssem.at[e], rsem.at[e], member(j)).start()
        pltpu.make_async_copy(out.at[e, part], into.at[e, part], rsem.at[e]).start()

    send_levels(0)

    ED = apply(quad(E), D)
    m4[3] = quad(E)
    m4[4] = quad(ED)
    m4[5] = quad(E, True)
    m4[6] = quad(-ED, True)
    m4[7] = quad(V)
    m4[8] = quad(DV)
    diagonal = lax.broadcasted_iota(jnp.int32, (64, 64), 0) == lanes((64, 64))
    column = jnp.sum(jnp.where(diagonal, jnp.broadcast_to(prof[...], (64, 64)), 0.0), axis=1, keepdims=True)
    profile = jnp.broadcast_to(column, (64, 128))

    halos[0].wait_recv()
    halos[1].wait_recv()
    halos[2].wait_recv()
    halos[3].wait_recv()
    loads[2].wait()

    def section(xp, carry):
        pair = []
        for x in (xp * 2, xp * 2 + 1):
            here = [velp[c, x + 1] for c in range(3)]
            rows = []
            for c in range(3):
                f = here[c]
                e, w = velp[c, x + 2], velp[c, x]
                j = c * 8 + x
                n = jnp.where(lane == 127, pltpu.roll(yhalo[1], 127 - j, 1), pltpu.roll(f, 127, 1))
                s = jnp.where(lane == 0, pltpu.roll(yhalo[0], (128 - j) % 128, 1), pltpu.roll(f, 1, 1))
                laplace = e + w + n + s - 4.0 * f
                lap[c, x] = laplace
                move = here[0] * (0.5 * (e - w)) + here[1] * (0.5 * (n - s))
                rows.append(f + step_weight * (coefv[x] * profile * laplace - move))
            pair.append((here, rows))
        for c in range(3):
            f = jnp.concatenate([pair[0][0][c], pair[1][0][c]], axis=1)
            slope = apply(m4[2], f)
            s = []
            for k in range(2):
                here, rows = pair[k]
                v = rows[c] - step_weight * (here[2] * slope[:, k * 128 : (k + 1) * 128])
                sec[c, xp * 2 + k] = v
                s.append(v)
            g = apply(m4[4 if c == 2 else 3], jnp.concatenate(s, axis=1))
            send_z[1, pl.ds(c * 8 + xp * 2, 64, stride=24), :] = g[:, :128]
            send_z[1, pl.ds(c * 8 + xp * 2 + 1, 64, stride=24), :] = g[:, 128:]
        return carry

    lax.fori_loop(0, 4, section, 0)
    send_levels(1, 0, CUT_F)

    for copy in loads[3:7]:
        copy.wait()

    kx_all = lax.broadcasted_iota(jnp.int32, (HALF, 128), 0).astype(f32) * UNIT

    def into_modes(e):
        all_of(recv_x.at[e], big_recv.at[e])
        g = [recv_x[e, :, c * 8 : (c + 1) * 8, :].reshape(N, 128) for c in range(3)]
        high, low = split(jnp.concatenate(g, axis=1))
        modes = dot3(tab[0], tab[1], high, low)
        c0, s0 = modes[:HALF, :128], modes[HALF:, :128]
        uc = modes[:HALF, 256:] + kx_all * s0
        us = modes[HALF:, 256:] - kx_all * c0
        vc, vs = modes[:HALF, 128:256], modes[HALF:, 128:256]
        for j in range(4):
            for r, block in enumerate((uc, us, vc, vs)):
                grp[e, j, r * 64 : (r + 1) * 64, :] = block[j * 64 : (j + 1) * 64]
        swap(e, grp, grp_in, grp_send, grp_recv)

    rate = rates[level]

    def solve(e):
        all_of(grp_in.at[e], grp_recv.at[e])
        high, low = split(jnp.concatenate([grp_in[e, j] for j in range(4)], axis=1))
        spec = dot3(high, low, ttab[0], ttab[1])
        row = lax.broadcasted_iota(jnp.int32, (128, HALF), 0) % 64 + part * 64
        kx = row.astype(f32) * UNIT
        ky = lanes((128, HALF)).astype(f32) * UNIT
        factor = -1.0 / (rate + kx * kx + ky * ky)
        pc = factor * (spec[:128, :HALF] + ky * spec[128:, HALF:])
        ps = factor * (spec[:128, HALF:] - ky * spec[128:, :HALF])
        both = jnp.concatenate(
            [
                jnp.concatenate([pc, ps], axis=1),
                jnp.concatenate([ky * ps, -(ky * pc)], axis=1),
            ],
            axis=0,
        )
        high, low = split(both)
        out = dot3(high, low, tab[0], tab[1])
        for j in range(4):
            bck[e, j] = out[:, j * 128 : (j + 1) * 128]
        swap(e, bck, bck_in, bck_send, bck_recv)

    def from_modes(e):
        all_of(bck_in.at[e], bck_recv.at[e])
        r = [
            jnp.concatenate([bck_in[e, j, k * 64 : (k + 1) * 64, :] for j in range(4)], axis=0)
            for k in range(4)
        ]
        pc, ps, yc, ys = r
        rhs = jnp.concatenate(
            [
                jnp.concatenate([kx_all * ps, yc, pc], axis=1),
                jnp.concatenate([-(kx_all * pc), ys, ps], axis=1),
            ],
            axis=0,
        )
        high, low = split(rhs)
        out = dot3(ttab[0], ttab[1], high, low)
        for c in range(3):
            back_x[e, :, c * 8 : (c + 1) * 8, :] = out[:, c * 128 : (c + 1) * 128].reshape(64, 8, 128)

    into_modes(0)
    send_levels(1, CUT_F, 64)
    solve(0)
    into_modes(1)
    from_modes(0)
    send_columns(0, 0, CUT_R)
    solve(1)
    send_columns(0, CUT_R, 64)
    from_modes(1)
    send_columns(1)

    all_of(back_z.at[0], ret_recv.at[0])

    def levels_of(e, c, x):
        return jnp.concatenate(
            [
                back_z[e, pl.ds(c * 8 + x, 64, stride=24), :],
                back_z[e, pl.ds(c * 8 + x + 1, 64, stride=24), :],
            ],
            axis=1,
        )

    def adjoint_out(xp, carry):
        x = xp * 2
        total = [zero, zero]
        for c in range(3):
            g = apply(m4[6 if c == 2 else 5], levels_of(0, c, x))
            for k in range(2):
                v = cotv[c, x + k] + g[:, k * 128 : (k + 1) * 128]
                cotv[c, x + k] = v
                total[k] = total[k] + v * lap[c, x + k]
        for k in range(2):
            grad[x + k] = step_weight * profile * total[k]
        return carry

    lax.fori_loop(0, 4, adjoint_out, 0)
    outs = [
        pltpu.make_async_copy(cotv, o_adj, out_sem.at[0]),
        pltpu.make_async_copy(grad, o_grad, out_sem.at[1]),
        pltpu.make_async_copy(sec, o_new, out_sem.at[2]),
    ]
    outs[0].start()
    outs[1].start()

    all_of(back_z.at[1], ret_recv.at[1])

    def forward_out(xp, carry):
        x = xp * 2
        for c in range(3):
            g = apply(m4[8 if c == 2 else 7], levels_of(1, c, x))
            for k in range(2):
                sec[c, x + k] = sec[c, x + k] - g[:, k * 128 : (k + 1) * 128]
        pltpu.make_async_copy(sec.at[:, pl.ds(x, 2)], o_new.at[:, pl.ds(x, 2)], out_sem.at[2]).start()
        return carry

    lax.fori_loop(0, 4, forward_out, 0)

    for copy in halos:
        copy.wait_send()
    for e in range(2):

        @pl.when(q == part)
        def _():
            all_of(recv_x.at[e, pl.ds(0, 63)], big_send.at[e])
            all_of(recv_x.at[e, pl.ds(0, 63)], ret_send.at[e])

        @pl.when(q != part)
        def _():
            all_of(recv_x.at[e], big_send.at[e])
            all_of(recv_x.at[e], ret_send.at[e])

        all_of(grp.at[e, pl.ds(0, 3)], grp_send.at[e])
        all_of(bck.at[e, pl.ds(0, 3)], bck_send.at[e])
    for copy in outs:
        copy.wait()


def place_kernel(a, b, c, to_a, to_b, to_c, va, vb, vc, sems):
    pieces = []
    for i in range(3):
        pieces.append((a.at[i], va.at[i], to_a.at[i]))
        pieces.append((b.at[i], vb.at[i], to_b.at[i]))
    pieces.append((c, vc, to_c))
    reads = [pltpu.make_async_copy(p[0], p[1], sems.at[0, i]) for i, p in enumerate(pieces)]
    writes = [pltpu.make_async_copy(p[1], p[2], sems.at[1, i]) for i, p in enumerate(pieces)]
    for copy in reads:
        copy.start()
    for read, write in zip(reads, writes):
        read.wait()
        write.start()
    for copy in writes:
        copy.wait()


def body(velocity, cotangent, coefficient, level_profile, vert_deriv, eigen_vectors, eigen_inverse, eigen_rates):
    tables = [jnp.asarray(t) for t in basis()]
    hbm = pl.BlockSpec(memory_space=pl.ANY)
    vmem = pl.BlockSpec(memory_space=pltpu.VMEM)
    smem = pl.BlockSpec(memory_space=pltpu.SMEM)
    field = (3, 8, 64, 128)
    dma = pltpu.SemaphoreType.DMA
    shapes = (
        jax.ShapeDtypeStruct(field, f32),
        jax.ShapeDtypeStruct(field, f32),
        jax.ShapeDtypeStruct(field[1:], f32),
    )
    results = pl.pallas_call(
        body_kernel,
        out_shape=shapes,
        in_specs=[hbm] * 6 + [vmem, smem] + [hbm] * 4,
        out_specs=(hbm, hbm, hbm),
        scratch_shapes=[
            pltpu.VMEM((3, 10, 64, 128), f32),
            pltpu.VMEM(field, f32),
            pltpu.VMEM(field[1:], f32),
            pltpu.VMEM(field, f32),
            pltpu.VMEM(field, f32),
            pltpu.VMEM(field[1:], f32),
            pltpu.VMEM((2, 64, 128), f32),
            pltpu.VMEM((2, 64, 128), f32),
            pltpu.VMEM((2, 1536, 128), f32),
            pltpu.VMEM((2, 64, 24, 128), f32),
            pltpu.VMEM((2, 64, 24, 128), f32),
            pltpu.VMEM((2, 1536, 128), f32),
            pltpu.VMEM((2, 4, 256, 128), f32),
            pltpu.VMEM((2, 4, 256, 128), f32),
            pltpu.VMEM((2, 4, 256, 128), f32),
            pltpu.VMEM((2, 4, 256, 128), f32),
            pltpu.VMEM((2, N, N), bf16),
            pltpu.VMEM((2, N, N), bf16),
            pltpu.VMEM((3, 64, 64), f32),
            pltpu.VMEM((9, 64, 256), bf16),
            dma((10,)),
            dma((3,)),
            dma((2,)), dma((2,)), dma((2,)), dma((2,)),
            dma((2,)), dma((2,)), dma((2,)), dma((2,)),
            dma((2,)), dma((2,)), dma((2,)), dma((2,)),
        ],
        compiler_params=pltpu.CompilerParams(
            collective_id=0, has_side_effects=True, vmem_limit_bytes=56 << 20
        ),
        name="substep",
    )(
        velocity, cotangent, coefficient, vert_deriv, eigen_vectors, eigen_inverse,
        level_profile[None, :], eigen_rates, *tables,
    )
    return pl.pallas_call(
        place_kernel,
        out_shape=shapes,
        in_specs=[hbm] * 3,
        out_specs=(hbm, hbm, hbm),
        scratch_shapes=[pltpu.VMEM(shape.shape, f32) for shape in shapes] + [dma((2, 7))],
        compiler_params=pltpu.CompilerParams(vmem_limit_bytes=56 << 20),
        name="place",
    )(*results)


def solution(mesh):
    field = P(None, "gx", None, "gy")
    cell = P("gx", None, "gy")
    in_specs = (field, field, cell, P(), P(), P(), P(), P())
    return jax.shard_map(body, mesh=mesh, in_specs=in_specs, out_specs=(field, field, cell), check_vma=False)
```
